32 devices in a mesh: ax: 8 (over z, x), rad: 4 (over y, core).
Axes of the slice: x: 2, y: 2, z: 4, core: 2. Of those that a mesh axis runs over, the one named last changes fastest.
Arguments:
- velocity: float32 [3, 12, 24, 768], P(None, 'rad', 'ax'), may hold values from -50 to 50
- cycle_map: int32 [3, 768], replicated, may hold values from 0 to 95, never falling along the last dimension, each value on 1 to 16 neighbouring positions
Outputs:
- new_velocity: float32 [3, 12, 24, 768], P(None, 'rad', 'ax')
The draws below stay inside these ranges and needn't reach their ends.
Inputs may be any that keep to these rules, and one draw needn't show every extreme that they name: `cycle_map`: in each row the numbers never fall along the azimuth, and each of 0 to 95 is taken by 1 to 16 consecutive points, one by exactly 16.
All inputs are finite; a program needn't handle non-finite values.
Results may differ from the reference program's by a relative error of at most 0.0003.
Values sent between devices are 32-bit elements; how exact they have to be, the bound alone decides.
A program may use at most 64 MiB of HBM per device.

```python
import math
import jax
import jax.numpy as jnp
import numpy as np
from jax import lax

TH = 768
Z_DEV = 3
NRING = 3
NC = 96
MOSTSEG = 16
NZ = 24
NR = 12
N_AX = 8


def box_along(values, axis, width):
    total = values
    for offset in range(1, width // 2 + 1):
        total = total + jnp.roll(values, offset, axis) + jnp.roll(values, -offset, axis)
    return total


def draw_velocity(key, part):
    subkeys = jax.random.split(key, 8)
    white_noise = jnp.clip(jax.random.normal(subkeys[0], (3, NR, NZ, TH), jnp.float32), -4.0, 4.0)
    other_noise = jnp.clip(jax.random.normal(subkeys[7], (3, NR, NZ, TH), jnp.float32), -4.0, 4.0)
    box_width = 5
    smooth_noise = box_along(box_along(other_noise, 2, box_width), 3, box_width) * (1.0 / box_width)
    block_of_row = jnp.arange(NZ, dtype=jnp.int32) * 8 // NZ
    block_order = jax.random.permutation(subkeys[4], 8).astype(jnp.float32)
    jitter = jax.random.uniform(subkeys[5], (8,), jnp.float32, 0.0, 1.0)
    white_share = 0.1 + 0.85 * (block_order + jitter) / 8.0
    block_gain = jnp.exp(jax.random.uniform(subkeys[6], (8,), jnp.float32, -1.0, 1.0) * 0.2)
    share_rows = white_share[block_of_row][None, None, :, None]
    rough_part = jnp.clip(jnp.sqrt(share_rows) * white_noise + jnp.sqrt(1.0 - share_rows) * smooth_noise, -3.0, 3.0)
    axial_pos = jnp.arange(NZ, dtype=jnp.float32) / NZ
    azimuth = jnp.arange(TH, dtype=jnp.float32) * (2.0 * math.pi / TH)
    radius = (jnp.arange(NR, dtype=jnp.float32) + 0.5) / NR
    phases = jax.random.uniform(subkeys[1], (3, 3), jnp.float32, 0.0, 2.0 * math.pi)
    smooth_part = 0.0
    for wave_number in range(3):
        smooth_part = smooth_part + jnp.sin(2.0 * math.pi * (wave_number + 1) * axial_pos[None, None, :, None] + (wave_number + 1) * azimuth[None, None, None, :] + 3.0 * radius[None, :, None, None] + phases[:, wave_number][:, None, None, None])
    row_scale = jnp.exp(jax.random.uniform(subkeys[2], (NZ,), jnp.float32, -1.0, 1.0) * (math.log(10.0) / 4.0))
    column_scale = jnp.exp(jax.random.uniform(subkeys[3], (TH,), jnp.float32, -1.0, 1.0) * (math.log(10.0) / 4.0))
    envelope = (1.0 + 2.0 * axial_pos) ** 0.25
    amplitude = (envelope * row_scale * block_gain[block_of_row])[None, None, :, None] * column_scale[None, None, None, :]
    mean_flow = 1.0 - radius * radius
    axial_mask = jnp.array([1.0, 0.0, 0.0], jnp.float32)
    mixed = rough_part + 2.0 * axial_pos[None, None, :, None] * smooth_part
    return amplitude * mixed + axial_mask[:, None, None, None] * mean_flow[None, :, None, None]


def profile(amount, total, limit, slope):
    loads = [(1 << 20) // math.isqrt(rank ** slope) + 1 for rank in range(2, amount + 1)]
    spare, given = total - limit - (amount - 1), [1] * (amount - 1)
    while spare > 0:
        free = [i for i in range(amount - 1) if given[i] < limit]
        pool, remaining = sum([loads[i] for i in free]), spare
        for i in free:
            more = min(limit - given[i], max(1, remaining * loads[i] // pool), spare)
            given[i] = given[i] + more
            spare = spare - more
    return np.array([limit] + given)


def uneven_parts(stream_key, number_of, total, most, lean):
    if number_of == 2:
        one = jax.random.randint(stream_key, (), max(1, total - most), min(most, total - 1) + 1)
        return jnp.stack([one, total - one])
    sizes = jnp.asarray(profile(number_of, total, most, lean), jnp.int32)
    twos = (number_of - 1) // 2
    donor, taker = sizes[1:1 + 2 * twos:2], sizes[2:2 + 2 * twos:2]
    slack = jnp.minimum(donor - 1, most - taker)
    moved = jax.random.randint(jax.random.fold_in(stream_key, 1), (twos,), 0, 1 << 20) % (slack + 1)
    sizes = sizes.at[1:1 + 2 * twos:2].set(donor - moved).at[2:2 + 2 * twos:2].set(taker + moved)
    return sizes[jax.random.permutation(jax.random.fold_in(stream_key, 2), number_of)]


def setup_inputs(seed: int = 0) -> dict:
    arg_keys = jax.random.split(jax.random.key(seed), 3)
    velocity = draw_velocity(jax.random.fold_in(arg_keys[2], 71), 0)
    cycle_map = jax.vmap(lambda own: jnp.searchsorted(jnp.cumsum(uneven_parts(own, NC, TH, MOSTSEG, 2)), jnp.arange(TH), side="right"))(jax.random.split(arg_keys[1], NRING)).reshape((NRING, TH)).astype(jnp.int32)
    return {"velocity": velocity, "cycle_map": cycle_map}


COMPONENT_PAIRS = ((0, 0), (1, 1), (2, 2), (0, 1), (0, 2), (1, 2))
PAIR_WEIGHTS = (1.0, 1.0, 1.0, 2.0, 2.0, 2.0)
VECTOR_SIGNS = (1.0, -1.0, -1.0)
TENSOR_SIGNS = (1.0, 1.0, 1.0, -1.0, -1.0, 1.0)
time_step = 1.0
epsilon = 1e-06

def pair_number(left_index, right_index):
    return COMPONENT_PAIRS.index((min(left_index, right_index), max(left_index, right_index)))

def trimmed(quantity, margin):
    if margin == 0:
        return quantity
    return quantity[margin:-margin, margin:-margin]

def central(quantity, direction):
    if direction == 0:
        return (quantity[1:-1, 2:] - quantity[1:-1, :-2]) * 0.5
    if direction == 1:
        return (quantity[2:, 1:-1] - quantity[:-2, 1:-1]) * 0.5
    shifted = (jnp.roll(quantity, -1, 2) - jnp.roll(quantity, 1, 2)) * 0.5
    return shifted[1:-1, 1:-1]

def test_filter(quantity):
    along_axis = (quantity[1:-1, :-2] + 2.0 * quantity[1:-1, 1:-1] + quantity[1:-1, 2:]) * 0.25
    return (jnp.roll(along_axis, 1, 2) + 2.0 * along_axis + jnp.roll(along_axis, -1, 2)) * 0.25

def strain_rate(velocity):
    gradient = [[central(velocity[component], direction) for direction in range(3)] for component in range(3)]
    tensor = [0.5 * (gradient[left_index][right_index] + gradient[right_index][left_index]) for left_index, right_index in COMPONENT_PAIRS]
    squares = sum((weight * member * member for weight, member in zip(PAIR_WEIGHTS, tensor)))
    return (tensor, jnp.sqrt(2.0 * squares))

def model_terms(velocity):
    tensor, magnitude = strain_rate(velocity)
    filtered = [test_filter(component) for component in velocity]
    tensor_hat, magnitude_hat = strain_rate(filtered)
    leonard_model = 0.0
    model_model = 0.0
    for number, (left_index, right_index) in enumerate(COMPONENT_PAIRS):
        product_hat = trimmed(test_filter(velocity[left_index] * velocity[right_index]), 1)
        leonard = product_hat - trimmed(filtered[left_index], 1) * trimmed(filtered[right_index], 1)
        model_term = test_filter(magnitude * tensor[number]) - 4.0 * magnitude_hat * tensor_hat[number]
        leonard_model = leonard_model + PAIR_WEIGHTS[number] * leonard * model_term
        model_model = model_model + PAIR_WEIGHTS[number] * model_term * model_term
    return (leonard_model, model_model, tensor, magnitude)

def flux_terms(velocity, tensor, magnitude, coefficient, margin_in, margin_out):
    speed_trim = margin_in - margin_out
    stress_trim = margin_in - 1 - margin_out
    viscosity = 2.0 * coefficient[:, None, None] * trimmed(magnitude, stress_trim)
    fluxes = []
    for number, (left_index, right_index) in enumerate(COMPONENT_PAIRS):
        advected = trimmed(velocity[left_index], speed_trim) * trimmed(velocity[right_index], speed_trim)
        fluxes.append(advected - viscosity * trimmed(tensor[number], stress_trim))
    return jnp.stack(fluxes)

def divergence(fluxes):
    tendencies = []
    for component in range(3):
        summed = 0.0
        for direction in range(3):
            summed = summed + central(fluxes[pair_number(component, direction)], direction)
        tendencies.append(-summed)
    return tendencies

def radial_rims(extended, rim_depth, rad_index, rad_count, sign_values):
    sign_column = jnp.asarray(sign_values, extended.dtype)[:, None, None, None]
    half_turn = extended.shape[3] // 2
    mirrored = sign_column * jnp.roll(extended[:, rim_depth:2 * rim_depth][:, ::-1], half_turn, 3)
    inner_rows = jnp.where(rad_index == 0, mirrored, extended[:, :rim_depth])
    outer_rows = jnp.where(rad_index == rad_count - 1, 0.0, extended[:, -rim_depth:])
    return jnp.concatenate([inner_rows, extended[:, rim_depth:-rim_depth], outer_rows], axis=1)

def coarsen_cycles(velocity, cycle_map):
    labels = jnp.arange(NC, dtype=jnp.int32)
    theta_points = velocity.shape[3]
    cycle_list = []
    for cycle_number in range(NRING):
        one_hot = (cycle_map[cycle_number][:, None] == labels[None, :]).astype(jnp.float32)
        cell_count = lax.optimization_barrier(jnp.sum(one_hot, axis=0))
        cycle_rows = velocity[:, cycle_number].reshape(-1, theta_points)
        cycle_sums = jnp.dot(cycle_rows, one_hot, precision=lax.Precision.HIGHEST, preferred_element_type=jnp.float32)
        cycle_means = cycle_sums / cell_count
        spread = jnp.dot(cycle_means, one_hot.T, precision=lax.Precision.HIGHEST, preferred_element_type=jnp.float32)
        cycle_list.append(spread.reshape(velocity[:, cycle_number].shape))
    return jnp.concatenate([jnp.stack(cycle_list, axis=1), velocity[:, NRING:]], axis=1)

def reference(velocity, cycle_map):
    coarse = coarsen_cycles(velocity, cycle_map)
    extended = radial_rims(jnp.pad(coarse, ((0, 0), (3, 3), (0, 0), (0, 0))), 3, 0, 1, VECTOR_SIGNS)
    total_z = extended.shape[2]

    def block_velocity(block):
        rows_z = (block * Z_DEV - 3 + jnp.arange(Z_DEV + 6, dtype=jnp.int32)) % total_z
        taken = jnp.take(extended, rows_z, axis=2)
        return [taken[0], taken[1], taken[2]]

    def coefficient_block(block):
        leonard_model, model_model, tensor, magnitude = model_terms(block_velocity(block))
        return (lax.optimization_barrier(jnp.sum(trimmed(leonard_model, 1), axis=(1, 2))), lax.optimization_barrier(jnp.sum(trimmed(model_model, 1), axis=(1, 2))))
    blocks = jnp.arange(N_AX, dtype=jnp.int32)
    lm_parts, mm_parts = lax.map(coefficient_block, blocks)
    cell_count = NZ * TH
    coefficient = lax.optimization_barrier(jnp.sum(lm_parts, axis=0)) / cell_count / (lax.optimization_barrier(jnp.sum(mm_parts, axis=0)) / cell_count + epsilon)
    coefficient_rows = jnp.pad(coefficient, 1)

    def update_block(block):
        components = block_velocity(block)
        tensor, magnitude = strain_rate(components)
        fluxes = flux_terms(components, tensor, magnitude, coefficient_rows, 3, 1)
        fluxes = radial_rims(fluxes, 1, 0, 1, TENSOR_SIGNS)
        tendencies = divergence(fluxes)
        return jnp.stack([trimmed(components[component], 3) + time_step * tendencies[component] for component in range(3)])
    result = lax.map(update_block, blocks)
    return jnp.transpose(result, (1, 2, 0, 3, 4)).reshape(3, NR, NZ, TH)
```

```python
import functools

import jax
import jax.numpy as jnp
from jax import lax
from jax.experimental import pallas as pl
from jax.experimental.pallas import tpu as pltpu
from jax.sharding import PartitionSpec as P

NRING = 3
MOSTSEG = 16
SUB = 8
LANES = 128
PAIRS = ((0, 0), (1, 1), (2, 2), (0, 1), (0, 2), (1, 2))
PAIR_WEIGHTS = (1.0, 1.0, 1.0, 2.0, 2.0, 2.0)
SIGNS = (1.0, -1.0, -1.0)
EPSILON = 1e-06
MESH = pl.DeviceIdType.MESH


def pair(a, b):
    return PAIRS.index((min(a, b), max(a, b)))


def each(count, body):
    if count <= 16:
        for i in range(count):
            body(i)
    else:
        lax.fori_loop(0, count, lambda i, c: (body(i), c)[1], 0)


def roll(x, shift, axis):
    size = x.shape[axis]
    return pltpu.roll(x, shift % size, axis)


def up(x):
    return roll(x, -1, x.ndim - 1)


def down(x):
    return roll(x, 1, x.ndim - 1)


def smooth_t(x):
    return (down(x) + 2.0 * x + up(x)) * 0.25


def smooth_z(x):
    return (x[:, :-2] + 2.0 * x[:, 1:-1] + x[:, 2:]) * 0.25


def segments(x, wide, pad):
    rows, total = x.shape
    tiles = total // LANES
    lane = lax.broadcasted_iota(jnp.int32, (rows, LANES), 1)
    pieces = []
    for s in range(SUB):
        start = (s * wide - pad) % total
        k, off = start // LANES, start % LANES
        first = x[:, k * LANES : (k + 1) * LANES]
        if off:
            k2 = (k + 1) % tiles
            second = x[:, k2 * LANES : (k2 + 1) * LANES]
            first = jnp.where(lane < LANES - off, roll(first, -off, 1), roll(second, -off, 1))
        pieces.append(first)
    return pieces


def joined(pieces, wide, pad):
    rows = pieces[0].shape[0]
    lane = lax.broadcasted_iota(jnp.int32, (rows, LANES), 1)
    tiles = []
    for k in range(SUB * wide // LANES):
        lo, hi = k * LANES, (k + 1) * LANES
        s = lo // wide
        out = None
        while s * wide < hi:
            part = roll(pieces[s], s * wide - pad - lo, 1)
            out = part if out is None else jnp.where(lane >= s * wide - lo, part, out)
            s += 1
        tiles.append(out)
    return tiles


def strain(grads):
    tensor = []
    for c, a in PAIRS:
        if c == a:
            tensor.append(0.5 * grads[c][c])
        else:
            tensor.append(0.25 * (grads[c][a] + grads[a][c]))
    squares = sum(w * m * m for w, m in zip(PAIR_WEIGHTS, tensor))
    return tensor, jnp.sqrt(2.0 * squares)


def gradients(f):
    out = []
    for c in range(3):
        mid = f[c][1:-1, 1:-1]
        out.append(
            [
                f[c][1:-1, 2:] - f[c][1:-1, :-2],
                f[c][2:, 1:-1] - f[c][:-2, 1:-1],
                up(mid) - down(mid),
            ]
        )
    return out


def kernel(n_ax, n_rad, v_ref, map_ref, out_ref, own, maps, ext, hx, part, parts, edge_coef,
           halo_send, halo_recv, h_send, h_recv, p_send, p_recv):
    rad = lax.axis_index("rad")
    ax = lax.axis_index("ax")
    R, Z, T = v_ref.shape[1], v_ref.shape[2], v_ref.shape[3]
    wide = T // SUB
    pad = (LANES - wide) // 2
    half = SUB // 2
    right, left = lax.rem(ax + 1, n_ax), lax.rem(ax + n_ax - 1, n_ax)
    has_lo, has_hi = rad > 0, rad < n_rad - 1

    barrier = pltpu.get_barrier_semaphore()

    def greet(to_rad, first):
        def body(i):
            peer = lax.rem(ax + first + i, n_ax)
            pl.semaphore_signal(barrier, inc=1, device_id=(peer, to_rad), device_id_type=MESH)
        each(n_ax - first, body)

    greet(rad, 1)
    pl.when(has_lo)(lambda: greet(rad - 1, 0))
    pl.when(has_hi)(lambda: greet(rad + 1, 0))

    for c in range(3):
        for r in range(R):
            for s, piece in enumerate(segments(v_ref[c, r], wide, pad)):
                own[pl.ds((c * R + r) * Z * SUB + s, Z, stride=SUB), :] = piece
    for c in range(3):
        for r in range(R):
            for z in range(Z):
                row = ((c * R + r) * Z + z) * SUB
                ext[c, r + 1, z + 2] = own[row : row + SUB, :]

    @pl.when(rad == 0)
    def _():
        labels = map_ref[...].astype(jnp.float32)
        for s, piece in enumerate(segments(labels, wide, pad)):
            maps[pl.ds(s, labels.shape[0], stride=SUB), :] = piece
        lane = lax.broadcasted_iota(jnp.int32, (SUB, LANES), 1)
        steps = []
        step = 1
        while step < MOSTSEG:
            steps.append(step)
            step *= 2
        for r in range(NRING):
            label = maps[r * SUB : (r + 1) * SUB, :]
            before = [(roll(label, d, 1) == label).astype(jnp.float32) for d in steps]
            after = [(roll(label, -d, 1) == label).astype(jnp.float32) for d in steps]

            def spread(x):
                total, rest = x, x
                for d, b, a in zip(steps, before, after):
                    total = total + b * roll(total, d, 1)
                    rest = rest + a * roll(rest, -d, 1)
                return total + rest - x

            inverse = 1.0 / spread(jnp.ones((SUB, LANES), jnp.float32))
            for c in range(3):
                for z in range(Z):
                    mean = spread(ext[c, r + 1, z + 2]) * inverse
                    low = roll(roll(mean, -wide, 1), 1, 0)
                    high = roll(roll(mean, wide, 1), -1, 0)
                    mean = jnp.where(lane < pad, low, mean)
                    mean = jnp.where(lane >= pad + wide, high, mean)
                    ext[c, r + 1, z + 2] = mean

    partners = n_ax - 1 + jnp.where(has_lo, n_ax, 0) + jnp.where(has_hi, n_ax, 0)
    pl.semaphore_wait(barrier, partners)

    rows, cols = pl.ds(1, R), pl.ds(2, Z)

    def halo(slot, src, dst, to_ax, to_rad):
        return pltpu.make_async_remote_copy(
            src_ref=ext.at[src], dst_ref=ext.at[dst], send_sem=halo_send.at[slot],
            recv_sem=halo_recv.at[slot], device_id=(to_ax, to_rad), device_id_type=MESH)

    everything = slice(None)
    z_lo = halo(0, (everything, rows, pl.ds(Z, 2)), (everything, rows, pl.ds(0, 2)), right, rad)
    z_hi = halo(1, (everything, rows, pl.ds(2, 2)), (everything, rows, pl.ds(Z + 2, 2)), left, rad)
    out_going = [
        halo(2, (everything, R, cols), (everything, 0, cols), ax, rad + 1),
        halo(3, (everything, R, Z + 1), (everything, 0, 1), right, rad + 1),
        halo(4, (everything, R, 2), (everything, 0, Z + 2), left, rad + 1),
    ]
    in_going = [
        halo(5, (everything, 1, cols), (everything, R + 1, cols), ax, rad - 1),
        halo(6, (everything, 1, Z + 1), (everything, R + 1, 1), right, rad - 1),
        halo(7, (everything, 1, 2), (everything, R + 1, Z + 2), left, rad - 1),
    ]

    z_lo.start()
    z_hi.start()

    def start_all(copies):
        for copy in copies:
            copy.start()

    def wait_recv(copies):
        for copy in copies:
            copy.wait_recv()

    def wait_send(copies):
        for copy in copies:
            copy.wait_send()

    pl.when(has_hi)(lambda: start_all(out_going))
    pl.when(has_lo)(lambda: start_all(in_going))
    wait_recv([z_lo, z_hi])
    pl.when(has_lo)(lambda: wait_recv(out_going))
    pl.when(has_hi)(lambda: wait_recv(in_going))

    @pl.when(rad == 0)
    def _():
        for c in range(3):
            for z in range(1, Z + 3):
                ext[c, 0, z] = SIGNS[c] * roll(ext[c, 1, z], half, 0)

    @pl.when(rad == n_rad - 1)
    def _():
        for c in range(3):
            for z in range(1, Z + 3):
                ext[c, R + 1, z] = jnp.zeros((SUB, LANES), jnp.float32)

    vel = [ext[c, 0 : R + 2, 1 : Z + 3] for c in range(3)]
    long = [ext[c, 1 : R + 1, 0 : Z + 4] for c in range(3)]
    grads = []
    for c in range(3):
        mid = vel[c][1:-1]
        grads.append([long[c][:, 2:] - long[c][:, :-2], vel[c][2:] - vel[c][:-2], up(mid) - down(mid)])
    tensor, mag = strain(grads)
    stress = [mag * t for t in tensor]
    w_own, w_lo, w_hi = [], [], []
    for c in range(3):
        w_own.append(smooth_t(smooth_z(long[c])))
        w_lo.append(smooth_t(smooth_z(vel[c][:1])))
        w_hi.append(smooth_t(smooth_z(vel[c][-1:])))
    w_grads = []
    for c in range(3):
        mid = w_own[c][:, 1:-1]
        column = jnp.concatenate([w_lo[c], mid, w_hi[c]], axis=0)
        w_grads.append([w_own[c][:, 2:] - w_own[c][:, :-2], column[2:] - column[:-2], up(mid) - down(mid)])
    w_tensor, w_mag = strain(w_grads)
    w_mag4 = 4.0 * w_mag
    lm, mm = 0.0, 0.0
    for number, (c, a) in enumerate(PAIRS):
        product = smooth_t(smooth_z(vel[c][1:-1] * vel[a][1:-1]))
        leonard = product - w_own[c][:, 1:-1] * w_own[a][:, 1:-1]
        model = smooth_t(smooth_z(stress[number])) - w_mag4 * w_tensor[number]
        lm = lm + PAIR_WEIGHTS[number] * leonard * model
        mm = mm + PAIR_WEIGHTS[number] * model * model
    sub_index = lax.broadcasted_iota(jnp.int32, (SUB, LANES), 0)
    lane_index = lax.broadcasted_iota(jnp.int32, (SUB, LANES), 1)
    mine = jnp.zeros((SUB, LANES), jnp.float32)
    for r in range(R):
        for base, quantity in ((0, lm), (half, mm)):
            row = jnp.sum(jnp.sum(quantity[r], axis=0), axis=0, keepdims=True)
            mine = jnp.where(sub_index == base + r, row, mine)
    mine = jnp.where((lane_index >= pad) & (lane_index < pad + wide), mine, 0.0)
    part[...] = mine

    def sums(side, i):
        peer = lax.rem(ax + i, n_ax)
        return pltpu.make_async_remote_copy(
            src_ref=part, dst_ref=parts.at[(1 - side) * n_ax + ax],
            send_sem=p_send.at[(1 + side) * n_ax + i], recv_sem=p_recv.at[(1 - side) * n_ax + ax],
            device_id=(peer, rad + side), device_id_type=MESH)

    def sums_in(side, i):
        peer = lax.rem(ax + i, n_ax)
        slot = (1 + side) * n_ax + peer
        return pltpu.make_async_remote_copy(
            src_ref=part, dst_ref=parts.at[slot],
            send_sem=p_send.at[(1 + side) * n_ax + i], recv_sem=p_recv.at[slot],
            device_id=(peer, rad + side), device_id_type=MESH)

    def first_of(side):
        return 1 if side == 0 else 0

    def send_sums(side):
        first = first_of(side)
        each(n_ax - first, lambda i: sums(side, i + first).start())

    send_sums(0)
    pl.when(has_lo)(lambda: send_sums(-1))
    pl.when(has_hi)(lambda: send_sums(1))

    for c in range(3):
        hx[c, 1 : R + 1] = stress[pair(c, 1)][:, 1:-1]

    def edge(slot, src, dst, to_rad):
        return pltpu.make_async_remote_copy(
            src_ref=hx.at[:, src], dst_ref=hx.at[:, dst], send_sem=h_send.at[slot],
            recv_sem=h_recv.at[slot], device_id=(ax, to_rad), device_id_type=MESH)

    edge_out = edge(0, R, 0, rad + 1)
    edge_in = edge(1, 1, R + 1, rad - 1)
    pl.when(has_hi)(lambda: edge_out.start())
    pl.when(has_lo)(lambda: edge_in.start())

    @pl.when(rad == 0)
    def _():
        for c in range(3):
            for z in range(Z):
                hx[c, 0, z] = SIGNS[c] * SIGNS[1] * roll(hx[c, 1, z], half, 0)

    @pl.when(rad == n_rad - 1)
    def _():
        for c in range(3):
            for z in range(Z):
                hx[c, R + 1, z] = jnp.zeros((SUB, LANES), jnp.float32)

    bases, turns = [], []
    for c in range(3):
        axial = vel[c][1:-1] * vel[0][1:-1]
        radial = vel[c][:, 1:-1] * vel[1][:, 1:-1]
        around = vel[c][1:-1, 1:-1] * vel[2][1:-1, 1:-1]
        change = axial[:, 2:] - axial[:, :-2] + (radial[2:] - radial[:-2]) + (up(around) - down(around))
        bases.append(vel[c][1:-1, 1:-1] - 0.5 * change)
        along = stress[pair(c, 0)]
        turn = stress[pair(c, 2)][:, 1:-1]
        turns.append(along[:, 2:] - along[:, :-2] + (up(turn) - down(turn)))

    count = n_ax * Z * T
    each(n_ax - 1, lambda i: sums_in(0, i + 1).wait_recv())

    def coefficients(total):
        total = jnp.broadcast_to(jnp.sum(total, axis=1, keepdims=True), (SUB, LANES)) / count
        return total / (roll(total, -half, 0) + EPSILON)

    def total_of(side):
        first = first_of(side)
        total = part[...] if first else jnp.zeros((SUB, LANES), jnp.float32)
        if n_ax <= 16:
            for i in range(first, n_ax):
                total = total + parts[(1 + side) * n_ax + lax.rem(ax + i, n_ax)]
            return total
        return lax.fori_loop(
            first, n_ax, lambda i, t: t + parts[(1 + side) * n_ax + lax.rem(ax + i, n_ax)], total)

    coef = coefficients(total_of(0))

    def beside(side, row):
        each(n_ax, lambda i: sums_in(side, i).wait_recv())
        edge_coef[0 if side < 0 else 1] = jnp.broadcast_to(
            coefficients(total_of(side))[row : row + 1], (SUB, LANES))

    pl.when(has_lo)(lambda: beside(-1, R - 1))
    pl.when(has_hi)(lambda: beside(1, 0))

    @pl.when(rad == 0)
    def _():
        edge_coef[0] = jnp.broadcast_to(coef[0:1], (SUB, LANES))

    @pl.when(rad == n_rad - 1)
    def _():
        edge_coef[1] = jnp.zeros((SUB, LANES), jnp.float32)

    pl.when(has_lo)(lambda: edge_out.wait_recv())
    pl.when(has_hi)(lambda: edge_in.wait_recv())
    by_row = [edge_coef[0]] + [jnp.broadcast_to(coef[r : r + 1], (SUB, LANES)) for r in range(R)] + [edge_coef[1]]
    for c in range(3):
        for r in range(R):
            new = bases[c][r] + by_row[r + 1] * turns[c][r]
            new = new + (by_row[r + 2] * hx[c, r + 2] - by_row[r] * hx[c, r])
            for z in range(Z):
                row = ((c * R + r) * Z + z) * SUB
                own[row : row + SUB, :] = new[z]
    for c in range(3):
        for r in range(R):
            pieces = [own[pl.ds((c * R + r) * Z * SUB + s, Z, stride=SUB), :] for s in range(SUB)]
            for k, tile in enumerate(joined(pieces, wide, pad)):
                out_ref[c, r, :, k * LANES : (k + 1) * LANES] = tile

    wait_send([z_lo, z_hi])

    @pl.when(has_hi)
    def _():
        wait_send(out_going + [edge_out])
        each(n_ax, lambda i: sums(1, i).wait_send())

    @pl.when(has_lo)
    def _():
        wait_send(in_going + [edge_in])
        each(n_ax, lambda i: sums(-1, i).wait_send())

    each(n_ax - 1, lambda i: sums(0, i + 1).wait_send())


def shards(n_ax, n_rad, velocity, cycle_map):
    _, R, Z, T = velocity.shape
    return pl.pallas_call(
        functools.partial(kernel, n_ax, n_rad),
        out_shape=jax.ShapeDtypeStruct(velocity.shape, velocity.dtype),
        in_specs=[pl.BlockSpec(memory_space=pltpu.VMEM)] * 2,
        out_specs=pl.BlockSpec(memory_space=pltpu.VMEM),
        scratch_shapes=[
            pltpu.VMEM((3 * R * Z * SUB, LANES), jnp.float32),
            pltpu.VMEM((NRING * SUB, LANES), jnp.float32),
            pltpu.VMEM((3, R + 2, Z + 4, SUB, LANES), jnp.float32),
            pltpu.VMEM((3, R + 2, Z, SUB, LANES), jnp.float32),
            pltpu.VMEM((SUB, LANES), jnp.float32),
            pltpu.VMEM((3 * n_ax, SUB, LANES), jnp.float32),
            pltpu.VMEM((2, SUB, LANES), jnp.float32),
            pltpu.SemaphoreType.DMA((8,)),
            pltpu.SemaphoreType.DMA((8,)),
            pltpu.SemaphoreType.DMA((2,)),
            pltpu.SemaphoreType.DMA((2,)),
            pltpu.SemaphoreType.DMA((3 * n_ax,)),
            pltpu.SemaphoreType.DMA((3 * n_ax,)),
        ],
        compiler_params=pltpu.CompilerParams(collective_id=0, has_side_effects=True),
    )(velocity, cycle_map)


def solution(mesh):
    n_ax, n_rad = mesh.shape["ax"], mesh.shape["rad"]
    spec = P(None, "rad", "ax", None)
    body = functools.partial(shards, n_ax, n_rad)
    return jax.shard_map(body, mesh=mesh, in_specs=(spec, P()), out_specs=spec, check_vma=False)
```

```python
import functools

import jax
import jax.numpy as jnp
from jax import lax
from jax.experimental import pallas as pl
from jax.experimental.pallas import tpu as pltpu
from jax.sharding import PartitionSpec as P

NRING = 3
MOSTSEG = 16
SUB = 8
LANES = 128
PAIRS = ((0, 0), (1, 1), (2, 2), (0, 1), (0, 2), (1, 2))
PAIR_WEIGHTS = (1.0, 1.0, 1.0, 2.0, 2.0, 2.0)
SIGNS = (1.0, -1.0, -1.0)
EPSILON = 1e-06
MESH = pl.DeviceIdType.MESH


def pair(a, b):
    return PAIRS.index((min(a, b), max(a, b)))


def each(count, body):
    if count <= 16:
        for i in range(count):
            body(i)
    else:
        lax.fori_loop(0, count, lambda i, c: (body(i), c)[1], 0)


def roll(x, shift, axis):
    size = x.shape[axis]
    return pltpu.roll(x, shift % size, axis)


def up(x):
    return roll(x, -1, x.ndim - 1)


def down(x):
    return roll(x, 1, x.ndim - 1)


def smooth_t(x):
    return (down(x) + 2.0 * x + up(x)) * 0.25


def smooth_z(x):
    return (x[:, :-2] + 2.0 * x[:, 1:-1] + x[:, 2:]) * 0.25


def tiles_of(x):
    return [x[:, k : k + LANES] for k in range(0, x.shape[1], LANES)]


def segments(x, wide, pad):
    rows, tiles = x[0].shape[0], len(x)
    total = tiles * LANES
    lane = lax.broadcasted_iota(jnp.int32, (rows, LANES), 1)
    pieces = []
    for s in range(SUB):
        start = (s * wide - pad) % total
        k, off = start // LANES, start % LANES
        first = x[k]
        if off:
            k2 = (k + 1) % tiles
            second = x[k2]
            first = jnp.where(lane < LANES - off, roll(first, -off, 1), roll(second, -off, 1))
        pieces.append(first)
    return pieces


def joined(pieces, wide, pad):
    rows = pieces[0].shape[0]
    lane = lax.broadcasted_iota(jnp.int32, (rows, LANES), 1)
    tiles = []
    for k in range(SUB * wide // LANES):
        lo, hi = k * LANES, (k + 1) * LANES
        s = lo // wide
        out = None
        while s * wide < hi:
            part = roll(pieces[s], s * wide - pad - lo, 1)
            out = part if out is None else jnp.where(lane >= s * wide - lo, part, out)
            s += 1
        tiles.append(out)
    return tiles


def strain(grads):
    tensor = []
    for c, a in PAIRS:
        if c == a:
            tensor.append(0.5 * grads[c][c])
        else:
            tensor.append(0.25 * (grads[c][a] + grads[a][c]))
    squares = sum(w * m * m for w, m in zip(PAIR_WEIGHTS, tensor))
    return tensor, jnp.sqrt(2.0 * squares)


def gradients(f):
    out = []
    for c in range(3):
        mid = f[c][1:-1, 1:-1]
        out.append(
            [
                f[c][1:-1, 2:] - f[c][1:-1, :-2],
                f[c][2:, 1:-1] - f[c][:-2, 1:-1],
                up(mid) - down(mid),
            ]
        )
    return out


def kernel(n_ax, n_rad, v_hbm, map_hbm, out_ref, nat, map_ref, own, maps, ext, hx, part, parts, edge_coef,
           z_out, z_in, z_seg, in_sems, halo_send, halo_recv, h_send, h_recv, p_send, p_recv):
    rad = lax.axis_index("rad")
    ax = lax.axis_index("ax")
    R, Z, T = nat.shape[1], nat.shape[2], nat.shape[3]
    wide = T // SUB
    pad = (LANES - wide) // 2
    half = SUB // 2
    right, left = lax.rem(ax + 1, n_ax), lax.rem(ax + n_ax - 1, n_ax)
    has_lo, has_hi = rad > 0, rad < n_rad - 1

    def strips(c, r):
        return [own[pl.ds((c * R + r) * Z * SUB + s, Z, stride=SUB), :] for s in range(SUB)]

    barrier = pltpu.get_barrier_semaphore()

    def greet(to_rad, first):
        def body(i):
            peer = lax.rem(ax + first + i, n_ax)
            pl.semaphore_signal(barrier, inc=1, device_id=(peer, to_rad), device_id_type=MESH)
        each(n_ax - first, body)

    greet(rad, 1)
    pl.when(has_lo)(lambda: greet(rad - 1, 0))
    pl.when(has_hi)(lambda: greet(rad + 1, 0))

    fetch = pltpu.make_async_copy(v_hbm, nat, in_sems.at[0])
    fetch.start()
    fetch_map = pltpu.make_async_copy(map_hbm, map_ref, in_sems.at[1])
    fetch_map.start()
    fetch.wait()
    fetch_map.wait()
    for c in range(3):
        for r in range(R):
            for s, piece in enumerate(segments(tiles_of(nat[c, r]), wide, pad)):
                own[pl.ds((c * R + r) * Z * SUB + s, Z, stride=SUB), :] = piece
    for c in range(3):
        for r in range(R):
            for z in range(Z):
                row = ((c * R + r) * Z + z) * SUB
                ext[c, r + 1, z + 2] = own[row : row + SUB, :]

    @pl.when(rad == 0)
    def _():
        labels = map_ref[...].astype(jnp.float32)
        for s, piece in enumerate(segments(tiles_of(labels), wide, pad)):
            maps[pl.ds(s, labels.shape[0], stride=SUB), :] = piece
        lane = lax.broadcasted_iota(jnp.int32, (SUB, LANES), 1)
        steps = []
        step = 1
        while step < MOSTSEG:
            steps.append(step)
            step *= 2
        for r in range(NRING):
            label = maps[r * SUB : (r + 1) * SUB, :]
            before = [(roll(label, d, 1) == label).astype(jnp.float32) for d in steps]
            after = [(roll(label, -d, 1) == label).astype(jnp.float32) for d in steps]

            def spread(x):
                total, rest = x, x
                for d, b, a in zip(steps, before, after):
                    total = total + b * roll(total, d, 1)
                    rest = rest + a * roll(rest, -d, 1)
                return total + rest - x

            inverse = 1.0 / spread(jnp.ones((SUB, LANES), jnp.float32))
            for c in range(3):
                for z in range(Z):
                    mean = spread(ext[c, r + 1, z + 2]) * inverse
                    low = roll(roll(mean, -wide, 1), 1, 0)
                    high = roll(roll(mean, wide, 1), -1, 0)
                    mean = jnp.where(lane < pad, low, mean)
                    mean = jnp.where(lane >= pad + wide, high, mean)
                    ext[c, r + 1, z + 2] = mean
                    row = ((c * R + r) * Z + z) * SUB
                    own[row : row + SUB, :] = mean
        for c in range(3):
            for r in range(NRING):
                for k, tile in enumerate(joined(strips(c, r), wide, pad)):
                    nat[c, r, :, k * LANES : (k + 1) * LANES] = tile

    n_rows = 3 * R * 2
    for side, first in ((0, Z - 2), (1, 0)):
        for c in range(3):
            for r in range(R):
                for k in range(T // LANES):
                    row = k * n_rows + (c * R + r) * 2
                    z_out[side, row : row + 2, :] = nat[c, r, first : first + 2, k * LANES : (k + 1) * LANES]

    partners = n_ax - 1 + jnp.where(has_lo, n_ax, 0) + jnp.where(has_hi, n_ax, 0)
    pl.semaphore_wait(barrier, partners)

    rows, cols = pl.ds(1, R), pl.ds(2, Z)

    def halo(slot, src, dst, to_ax, to_rad):
        return pltpu.make_async_remote_copy(
            src_ref=ext.at[src], dst_ref=ext.at[dst], send_sem=halo_send.at[slot],
            recv_sem=halo_recv.at[slot], device_id=(to_ax, to_rad), device_id_type=MESH)

    everything = slice(None)

    def z_halo(slot, to_ax):
        return pltpu.make_async_remote_copy(
            src_ref=z_out.at[slot], dst_ref=z_in.at[slot], send_sem=halo_send.at[slot],
            recv_sem=halo_recv.at[slot], device_id=(to_ax, rad), device_id_type=MESH)

    z_lo, z_hi = z_halo(0, right), z_halo(1, left)
    out_going = [
        halo(2, (everything, R, cols), (everything, 0, cols), ax, rad + 1),
        halo(3, (everything, R, Z + 1), (everything, 0, 1), right, rad + 1),
        halo(4, (everything, R, 2), (everything, 0, Z + 2), left, rad + 1),
    ]
    in_going = [
        halo(5, (everything, 1, cols), (everything, R + 1, cols), ax, rad - 1),
        halo(6, (everything, 1, Z + 1), (everything, R + 1, 1), right, rad - 1),
        halo(7, (everything, 1, 2), (everything, R + 1, Z + 2), left, rad - 1),
    ]

    z_lo.start()
    z_hi.start()

    def start_all(copies):
        for copy in copies:
            copy.start()

    def wait_recv(copies):
        for copy in copies:
            copy.wait_recv()

    def wait_send(copies):
        for copy in copies:
            copy.wait_send()

    pl.when(has_hi)(lambda: start_all(out_going))
    pl.when(has_lo)(lambda: start_all(in_going))
    for side, copy, first in ((0, z_lo, 0), (1, z_hi, Z + 2)):
        copy.wait_recv()
        tiles = [z_in[side, k * n_rows : (k + 1) * n_rows, :] for k in range(T // LANES)]
        for s, piece in enumerate(segments(tiles, wide, pad)):
            z_seg[pl.ds(side * n_rows * SUB + s, n_rows, stride=SUB), :] = piece
        for c in range(3):
            for r in range(R):
                for z in range(2):
                    row = (side * n_rows + (c * R + r) * 2 + z) * SUB
                    ext[c, r + 1, first + z] = z_seg[row : row + SUB, :]
    pl.when(has_lo)(lambda: wait_recv(out_going))
    pl.when(has_hi)(lambda: wait_recv(in_going))

    @pl.when(rad == 0)
    def _():
        for c in range(3):
            for z in range(1, Z + 3):
                ext[c, 0, z] = SIGNS[c] * roll(ext[c, 1, z], half, 0)

    @pl.when(rad == n_rad - 1)
    def _():
        for c in range(3):
            for z in range(1, Z + 3):
                ext[c, R + 1, z] = jnp.zeros((SUB, LANES), jnp.float32)

    vel = [ext[c, 0 : R + 2, 1 : Z + 3] for c in range(3)]
    long = [ext[c, 1 : R + 1, 0 : Z + 4] for c in range(3)]
    grads = []
    for c in range(3):
        mid = vel[c][1:-1]
        grads.append([long[c][:, 2:] - long[c][:, :-2], vel[c][2:] - vel[c][:-2], up(mid) - down(mid)])
    tensor, mag = strain(grads)
    stress = [mag * t for t in tensor]
    w_own, w_lo, w_hi = [], [], []
    for c in range(3):
        w_own.append(smooth_t(smooth_z(long[c])))
        w_lo.append(smooth_t(smooth_z(vel[c][:1])))
        w_hi.append(smooth_t(smooth_z(vel[c][-1:])))
    w_grads = []
    for c in range(3):
        mid = w_own[c][:, 1:-1]
        column = jnp.concatenate([w_lo[c], mid, w_hi[c]], axis=0)
        w_grads.append([w_own[c][:, 2:] - w_own[c][:, :-2], column[2:] - column[:-2], up(mid) - down(mid)])
    w_tensor, w_mag = strain(w_grads)
    w_mag4 = 4.0 * w_mag
    lm, mm = 0.0, 0.0
    for number, (c, a) in enumerate(PAIRS):
        product = smooth_t(smooth_z(vel[c][1:-1] * vel[a][1:-1]))
        leonard = product - w_own[c][:, 1:-1] * w_own[a][:, 1:-1]
        model = smooth_t(smooth_z(stress[number])) - w_mag4 * w_tensor[number]
        lm = lm + PAIR_WEIGHTS[number] * leonard * model
        mm = mm + PAIR_WEIGHTS[number] * model * model
    sub_index = lax.broadcasted_iota(jnp.int32, (SUB, LANES), 0)
    lane_index = lax.broadcasted_iota(jnp.int32, (SUB, LANES), 1)
    mine = jnp.zeros((SUB, LANES), jnp.float32)
    for r in range(R):
        for base, quantity in ((0, lm), (half, mm)):
            row = jnp.sum(jnp.sum(quantity[r], axis=0), axis=0, keepdims=True)
            mine = jnp.where(sub_index == base + r, row, mine)
    mine = jnp.where((lane_index >= pad) & (lane_index < pad + wide), mine, 0.0)
    fold = LANES // 2
    while fold >= LANES // SUB:
        mine = mine + roll(mine, fold, 1)
        fold //= 2
    group = lane_index // (LANES // SUB) == sub_index
    part[...] = jnp.sum(jnp.where(group, mine, 0.0), axis=0, keepdims=True)

    def sums(side, i):
        peer = lax.rem(ax + i, n_ax)
        return pltpu.make_async_remote_copy(
            src_ref=part, dst_ref=parts.at[(1 - side) * n_ax + ax],
            send_sem=p_send.at[(1 + side) * n_ax + i], recv_sem=p_recv.at[(1 - side) * n_ax + ax],
            device_id=(peer, rad + side), device_id_type=MESH)

    def sums_in(side, i):
        peer = lax.rem(ax + i, n_ax)
        slot = (1 + side) * n_ax + peer
        return pltpu.make_async_remote_copy(
            src_ref=part, dst_ref=parts.at[slot],
            send_sem=p_send.at[(1 + side) * n_ax + i], recv_sem=p_recv.at[slot],
            device_id=(peer, rad + side), device_id_type=MESH)

    def first_of(side):
        return 1 if side == 0 else 0

    def send_sums(side):
        first = first_of(side)
        each(n_ax - first, lambda i: sums(side, i + first).start())

    send_sums(0)
    pl.when(has_lo)(lambda: send_sums(-1))
    pl.when(has_hi)(lambda: send_sums(1))

    for c in range(3):
        hx[c, 1 : R + 1] = stress[pair(c, 1)][:, 1:-1]

    def edge(slot, src, dst, to_rad):
        return pltpu.make_async_remote_copy(
            src_ref=hx.at[:, src], dst_ref=hx.at[:, dst], send_sem=h_send.at[slot],
            recv_sem=h_recv.at[slot], device_id=(ax, to_rad), device_id_type=MESH)

    edge_out = edge(0, R, 0, rad + 1)
    edge_in = edge(1, 1, R + 1, rad - 1)
    pl.when(has_hi)(lambda: edge_out.start())
    pl.when(has_lo)(lambda: edge_in.start())

    @pl.when(rad == 0)
    def _():
        for c in range(3):
            for z in range(Z):
                hx[c, 0, z] = SIGNS[c] * SIGNS[1] * roll(hx[c, 1, z], half, 0)

    @pl.when(rad == n_rad - 1)
    def _():
        for c in range(3):
            for z in range(Z):
                hx[c, R + 1, z] = jnp.zeros((SUB, LANES), jnp.float32)

    bases, turns = [], []
    for c in range(3):
        axial = vel[c][1:-1] * vel[0][1:-1]
        radial = vel[c][:, 1:-1] * vel[1][:, 1:-1]
        around = vel[c][1:-1, 1:-1] * vel[2][1:-1, 1:-1]
        change = axial[:, 2:] - axial[:, :-2] + (radial[2:] - radial[:-2]) + (up(around) - down(around))
        bases.append(vel[c][1:-1, 1:-1] - 0.5 * change)
        along = stress[pair(c, 0)]
        turn = stress[pair(c, 2)][:, 1:-1]
        turns.append(along[:, 2:] - along[:, :-2] + (up(turn) - down(turn)))

    count = n_ax * Z * T
    each(n_ax - 1, lambda i: sums_in(0, i + 1).wait_recv())

    def coefficients(total):
        total = jnp.broadcast_to(jnp.sum(jnp.where(group, total, 0.0), axis=1, keepdims=True), (SUB, LANES)) / count
        return total / (roll(total, -half, 0) + EPSILON)

    def total_of(side):
        first = first_of(side)
        total = part[...] if first else jnp.zeros((1, LANES), jnp.float32)
        if n_ax <= 16:
            for i in range(first, n_ax):
                total = total + parts[(1 + side) * n_ax + lax.rem(ax + i, n_ax)]
            return total
        return lax.fori_loop(
            first, n_ax, lambda i, t: t + parts[(1 + side) * n_ax + lax.rem(ax + i, n_ax)], total)

    coef = coefficients(total_of(0))

    def beside(side, row):
        each(n_ax, lambda i: sums_in(side, i).wait_recv())
        edge_coef[0 if side < 0 else 1] = jnp.broadcast_to(
            coefficients(total_of(side))[row : row + 1], (SUB, LANES))

    pl.when(has_lo)(lambda: beside(-1, R - 1))
    pl.when(has_hi)(lambda: beside(1, 0))

    @pl.when(rad == 0)
    def _():
        edge_coef[0] = jnp.broadcast_to(coef[0:1], (SUB, LANES))

    @pl.when(rad == n_rad - 1)
    def _():
        edge_coef[1] = jnp.zeros((SUB, LANES), jnp.float32)

    pl.when(has_lo)(lambda: edge_out.wait_recv())
    pl.when(has_hi)(lambda: edge_in.wait_recv())
    by_row = [edge_coef[0]] + [jnp.broadcast_to(coef[r : r + 1], (SUB, LANES)) for r in range(R)] + [edge_coef[1]]
    for c in range(3):
        for r in range(R):
            new = bases[c][r] + by_row[r + 1] * turns[c][r]
            new = new + (by_row[r + 2] * hx[c, r + 2] - by_row[r] * hx[c, r])
            for z in range(Z):
                row = ((c * R + r) * Z + z) * SUB
                own[row : row + SUB, :] = new[z]
    for c in range(3):
        for r in range(R):
            for k, tile in enumerate(joined(strips(c, r), wide, pad)):
                out_ref[c, r, :, k * LANES : (k + 1) * LANES] = tile

    wait_send([z_lo, z_hi])

    @pl.when(has_hi)
    def _():
        wait_send(out_going + [edge_out])
        each(n_ax, lambda i: sums(1, i).wait_send())

    @pl.when(has_lo)
    def _():
        wait_send(in_going + [edge_in])
        each(n_ax, lambda i: sums(-1, i).wait_send())

    each(n_ax - 1, lambda i: sums(0, i + 1).wait_send())


def shards(n_ax, n_rad, velocity, cycle_map):
    _, R, Z, T = velocity.shape
    return pl.pallas_call(
        functools.partial(kernel, n_ax, n_rad),
        out_shape=jax.ShapeDtypeStruct(velocity.shape, velocity.dtype),
        in_specs=[pl.BlockSpec(memory_space=pltpu.HBM)] * 2,
        out_specs=pl.BlockSpec(memory_space=pltpu.VMEM),
        scratch_shapes=[
            pltpu.VMEM(velocity.shape, jnp.float32),
            pltpu.VMEM(cycle_map.shape, jnp.int32),
            pltpu.VMEM((3 * R * Z * SUB, LANES), jnp.float32),
            pltpu.VMEM((NRING * SUB, LANES), jnp.float32),
            pltpu.VMEM((3, R + 2, Z + 4, SUB, LANES), jnp.float32),
            pltpu.VMEM((3, R + 2, Z, SUB, LANES), jnp.float32),
            pltpu.VMEM((1, LANES), jnp.float32),
            pltpu.VMEM((3 * n_ax, 1, LANES), jnp.float32),
            pltpu.VMEM((2, SUB, LANES), jnp.float32),
            pltpu.VMEM((2, 3 * R * 2 * T // LANES, LANES), jnp.float32),
            pltpu.VMEM((2, 3 * R * 2 * T // LANES, LANES), jnp.float32),
            pltpu.VMEM((2 * 3 * R * 2 * SUB, LANES), jnp.float32),
            pltpu.SemaphoreType.DMA((2,)),
            pltpu.SemaphoreType.DMA((8,)),
            pltpu.SemaphoreType.DMA((8,)),
            pltpu.SemaphoreType.DMA((2,)),
            pltpu.SemaphoreType.DMA((2,)),
            pltpu.SemaphoreType.DMA((3 * n_ax,)),
            pltpu.SemaphoreType.DMA((3 * n_ax,)),
        ],
        compiler_params=pltpu.CompilerParams(collective_id=0, has_side_effects=True, vmem_limit_bytes=8 << 20),
    )(*(pltpu.with_memory_space_constraint(x, pltpu.HBM) for x in (velocity, cycle_map)))


def solution(mesh):
    n_ax, n_rad = mesh.shape["ax"], mesh.shape["rad"]
    spec = P(None, "rad", "ax", None)
    body = functools.partial(shards, n_ax, n_rad)
    return jax.shard_map(body, mesh=mesh, in_specs=(spec, P()), out_specs=spec, check_vma=False)
```

```python
import functools

import jax
import jax.numpy as jnp
from jax import lax
from jax.experimental import pallas as pl
from jax.experimental.pallas import tpu as pltpu
from jax.sharding import PartitionSpec as P

NRING = 3
MOSTSEG = 16
SUB = 8
LANES = 128
PAIRS = ((0, 0), (1, 1), (2, 2), (0, 1), (0, 2), (1, 2))
PAIR_WEIGHTS = (1.0, 1.0, 1.0, 2.0, 2.0, 2.0)
SIGNS = (1.0, -1.0, -1.0)
EPSILON = 1e-06
MESH = pl.DeviceIdType.MESH


def pair(a, b):
    return PAIRS.index((min(a, b), max(a, b)))


def each(count, body):
    if count <= 16:
        for i in range(count):
            body(i)
    else:
        lax.fori_loop(0, count, lambda i, c: (body(i), c)[1], 0)


def roll(x, shift, axis):
    size = x.shape[axis]
    return pltpu.roll(x, shift % size, axis)


def up(x):
    return roll(x, -1, x.ndim - 1)


def down(x):
    return roll(x, 1, x.ndim - 1)


def smooth_t(x):
    return (down(x) + 2.0 * x + up(x)) * 0.25


def smooth_z(x):
    return (x[:, :-2] + 2.0 * x[:, 1:-1] + x[:, 2:]) * 0.25


def tiles_of(x):
    return [x[:, k : k + LANES] for k in range(0, x.shape[1], LANES)]


def segments(x, wide, pad):
    rows, tiles = x[0].shape[0], len(x)
    total = tiles * LANES
    lane = lax.broadcasted_iota(jnp.int32, (rows, LANES), 1)
    pieces = []
    for s in range(SUB):
        start = (s * wide - pad) % total
        k, off = start // LANES, start % LANES
        first = x[k]
        if off:
            k2 = (k + 1) % tiles
            second = x[k2]
            first = jnp.where(lane < LANES - off, roll(first, -off, 1), roll(second, -off, 1))
        pieces.append(first)
    return pieces


def joined(pieces, wide, pad):
    rows = pieces[0].shape[0]
    lane = lax.broadcasted_iota(jnp.int32, (rows, LANES), 1)
    tiles = []
    for k in range(SUB * wide // LANES):
        lo, hi = k * LANES, (k + 1) * LANES
        s = lo // wide
        out = None
        while s * wide < hi:
            part = roll(pieces[s], s * wide - pad - lo, 1)
            out = part if out is None else jnp.where(lane >= s * wide - lo, part, out)
            s += 1
        tiles.append(out)
    return tiles


def strain(grads):
    tensor = []
    for c, a in PAIRS:
        if c == a:
            tensor.append(0.5 * grads[c][c])
        else:
            tensor.append(0.25 * (grads[c][a] + grads[a][c]))
    squares = sum(w * m * m for w, m in zip(PAIR_WEIGHTS, tensor))
    return tensor, jnp.sqrt(2.0 * squares)


def gradients(f):
    out = []
    for c in range(3):
        mid = f[c][1:-1, 1:-1]
        out.append(
            [
                f[c][1:-1, 2:] - f[c][1:-1, :-2],
                f[c][2:, 1:-1] - f[c][:-2, 1:-1],
                up(mid) - down(mid),
            ]
        )
    return out


def stages(n_ax):
    distances, own, beside = [1], 2, 1
    while own < n_ax // 2:
        distances.append(own)
        own, beside = 2 * own, beside + own
    while beside < n_ax // 2:
        distances.append(1)
        beside += 1
    return distances


def kernel(n_ax, n_rad, v_hbm, map_hbm, out_ref, nat, map_ref, own, maps, ext, hx, part, parts, edge_coef,
           z_out, z_in, z_seg, ready, in_sems, halo_send, halo_recv, h_send, h_recv, p_send, p_recv):
    rad = lax.axis_index("rad")
    ax = lax.axis_index("ax")
    R, Z, T = nat.shape[1], nat.shape[2], nat.shape[3]
    wide = T // SUB
    pad = (LANES - wide) // 2
    half = SUB // 2
    right, left = lax.rem(ax + 1, n_ax), lax.rem(ax + n_ax - 1, n_ax)
    has_lo, has_hi = rad > 0, rad < n_rad - 1

    def strips(c, r):
        return [own[pl.ds((c * R + r) * Z * SUB + s, Z, stride=SUB), :] for s in range(SUB)]

    barrier = pltpu.get_barrier_semaphore()

    def greet(to_ax, to_rad):
        pl.semaphore_signal(barrier, inc=1, device_id=(to_ax, to_rad), device_id_type=MESH)

    greet(left, rad)
    greet(right, rad)
    pl.when(has_lo)(lambda: greet(ax, rad - 1))
    pl.when(has_hi)(lambda: greet(ax, rad + 1))

    distances = stages(n_ax)

    def tell(stage):
        d = distances[stage]
        for peer in (lax.rem(ax + d, n_ax), lax.rem(ax + n_ax - d, n_ax)):
            pl.semaphore_signal(ready.at[stage], inc=1, device_id=(peer, rad), device_id_type=MESH)

    def hear(stage):
        pl.semaphore_wait(ready.at[stage], 2)

    fetch = pltpu.make_async_copy(v_hbm, nat, in_sems.at[0])
    fetch.start()
    fetch_map = pltpu.make_async_copy(map_hbm, map_ref, in_sems.at[1])
    pl.when(rad == 0)(lambda: fetch_map.start())
    fetch.wait()
    n_rows = 3 * R * 2
    for side, first in ((0, Z - 2), (1, 0)):
        for c in range(3):
            for r in range(R):
                for k in range(T // LANES):
                    row = k * n_rows + (c * R + r) * 2
                    z_out[side, row : row + 2, :] = nat[c, r, first : first + 2, k * LANES : (k + 1) * LANES]

    pl.semaphore_wait(barrier, 2 + jnp.where(has_lo, 1, 0) + jnp.where(has_hi, 1, 0))

    def z_halo(slot, to_ax):
        return pltpu.make_async_remote_copy(
            src_ref=z_out.at[slot], dst_ref=z_in.at[slot], send_sem=halo_send.at[slot],
            recv_sem=halo_recv.at[slot], device_id=(to_ax, rad), device_id_type=MESH)

    z_lo, z_hi = z_halo(0, right), z_halo(1, left)
    z_lo.start()
    z_hi.start()
    tell(0)

    for c in range(3):
        for r in range(R):
            for s, piece in enumerate(segments(tiles_of(nat[c, r]), wide, pad)):
                own[pl.ds((c * R + r) * Z * SUB + s, Z, stride=SUB), :] = piece
    for c in range(3):
        for r in range(R):
            for z in range(Z):
                row = ((c * R + r) * Z + z) * SUB
                ext[c, r + 1, z + 2] = own[row : row + SUB, :]

    lane = lax.broadcasted_iota(jnp.int32, (SUB, LANES), 1)
    steps = []
    while 2 ** len(steps) < MOSTSEG:
        steps.append(2 ** len(steps))

    def cell_sums(r):
        label = maps[r * SUB : (r + 1) * SUB, :]
        before = [(roll(label, d, 1) == label).astype(jnp.float32) for d in steps]
        after = [(roll(label, -d, 1) == label).astype(jnp.float32) for d in steps]

        def spread(x):
            total, rest = x, x
            for d, b, a in zip(steps, before, after):
                total = total + b * roll(total, d, 1)
                rest = rest + a * roll(rest, -d, 1)
            return total + rest - x

        return spread

    def coarsen(r, spread, c, z):
        mean = spread(ext[c, r + 1, z]) * maps[(NRING + r) * SUB : (NRING + r + 1) * SUB, :]
        low = roll(roll(mean, -wide, 1), 1, 0)
        high = roll(roll(mean, wide, 1), -1, 0)
        mean = jnp.where(lane < pad, low, mean)
        ext[c, r + 1, z] = jnp.where(lane >= pad + wide, high, mean)

    @pl.when(rad == 0)
    def _():
        fetch_map.wait()
        labels = map_ref[...].astype(jnp.float32)
        for s, piece in enumerate(segments(tiles_of(labels), wide, pad)):
            maps[pl.ds(s, NRING, stride=SUB), :] = piece
        for r in range(NRING):
            spread = cell_sums(r)
            maps[(NRING + r) * SUB : (NRING + r + 1) * SUB, :] = 1.0 / spread(jnp.ones((SUB, LANES), jnp.float32))
            for c in range(3):
                for z in range(Z):
                    coarsen(r, spread, c, z + 2)

    rows, cols = pl.ds(1, R), pl.ds(2, Z)

    def halo(slot, src, dst, to_ax, to_rad):
        return pltpu.make_async_remote_copy(
            src_ref=ext.at[src], dst_ref=ext.at[dst], send_sem=halo_send.at[slot],
            recv_sem=halo_recv.at[slot], device_id=(to_ax, to_rad), device_id_type=MESH)

    everything = slice(None)

    out_going = [
        halo(2, (everything, R, cols), (everything, 0, cols), ax, rad + 1),
        halo(3, (everything, R, Z + 1), (everything, 0, 1), right, rad + 1),
        halo(4, (everything, R, 2), (everything, 0, Z + 2), left, rad + 1),
    ]
    in_going = [
        halo(5, (everything, 1, cols), (everything, R + 1, cols), ax, rad - 1),
        halo(6, (everything, 1, Z + 1), (everything, R + 1, 1), right, rad - 1),
        halo(7, (everything, 1, 2), (everything, R + 1, Z + 2), left, rad - 1),
    ]

    def start_all(copies):
        for copy in copies:
            copy.start()

    def wait_recv(copies):
        for copy in copies:
            copy.wait_recv()

    def wait_send(copies):
        for copy in copies:
            copy.wait_send()

    pl.when(has_hi)(lambda: start_all(out_going[:1]))
    pl.when(has_lo)(lambda: start_all(in_going[:1]))
    for stage in range(len(distances) - 1)[:1]:
        hear(stage)
        tell(stage + 1)
    pl.when(has_hi)(lambda: start_all(out_going[1:]))
    pl.when(has_lo)(lambda: start_all(in_going[1:]))
    for side, copy, first in ((0, z_lo, 0), (1, z_hi, Z + 2)):
        copy.wait_recv()
        tiles = [z_in[side, k * n_rows : (k + 1) * n_rows, :] for k in range(T // LANES)]
        for s, piece in enumerate(segments(tiles, wide, pad)):
            z_seg[pl.ds(side * n_rows * SUB + s, n_rows, stride=SUB), :] = piece
        for c in range(3):
            for r in range(R):
                for z in range(2):
                    row = (side * n_rows + (c * R + r) * 2 + z) * SUB
                    ext[c, r + 1, first + z] = z_seg[row : row + SUB, :]
    @pl.when(rad == 0)
    def _():
        for r in range(NRING):
            spread = cell_sums(r)
            for c in range(3):
                for z in (0, 1, Z + 2, Z + 3):
                    coarsen(r, spread, c, z)

    for stage in range(1, len(distances) - 1):
        hear(stage)
        tell(stage + 1)

    long = [ext[c, 1 : R + 1, 0 : Z + 4] for c in range(3)]
    mids = [x[:, 1:-1] for x in long]
    grads, w_own, w_grads, leonards = [], [], [], []
    for c in range(3):
        turned = up(mids[c]) - down(mids[c])
        grads.append([long[c][:, 2:] - long[c][:, :-2], None, turned])
        w_own.append(smooth_t(smooth_z(long[c])))
        mid = w_own[c][:, 1:-1]
        w_grads.append([w_own[c][:, 2:] - w_own[c][:, :-2], None, up(mid) - down(mid)])
    for c, a in PAIRS:
        product = smooth_t(smooth_z(mids[c] * mids[a]))
        leonards.append(product - w_own[c][:, 1:-1] * w_own[a][:, 1:-1])

    pl.when(has_lo)(lambda: wait_recv(out_going))
    pl.when(has_hi)(lambda: wait_recv(in_going))

    @pl.when(rad == 0)
    def _():
        for c in range(3):
            for z in range(1, Z + 3):
                ext[c, 0, z] = SIGNS[c] * roll(ext[c, 1, z], half, 0)

    @pl.when(rad == n_rad - 1)
    def _():
        for c in range(3):
            for z in range(1, Z + 3):
                ext[c, R + 1, z] = jnp.zeros((SUB, LANES), jnp.float32)

    below = [ext[c, 0:1, 1 : Z + 3] for c in range(3)]
    above = [ext[c, R + 1 : R + 2, 1 : Z + 3] for c in range(3)]
    for c in range(3):
        column = jnp.concatenate([below[c], mids[c], above[c]], axis=0)
        grads[c][1] = column[2:] - column[:-2]
        column = jnp.concatenate(
            [smooth_t(smooth_z(below[c])), w_own[c][:, 1:-1], smooth_t(smooth_z(above[c]))], axis=0)
        w_grads[c][1] = column[2:] - column[:-2]
    tensor, mag = strain(grads)
    stress = [mag * t for t in tensor]
    w_tensor, w_mag = strain(w_grads)
    w_mag4 = 4.0 * w_mag
    lm, mm = 0.0, 0.0
    for number, leonard in enumerate(leonards):
        model = smooth_t(smooth_z(stress[number])) - w_mag4 * w_tensor[number]
        lm = lm + PAIR_WEIGHTS[number] * leonard * model
        mm = mm + PAIR_WEIGHTS[number] * model * model
    sub_index = lax.broadcasted_iota(jnp.int32, (SUB, LANES), 0)
    lane_index = lax.broadcasted_iota(jnp.int32, (SUB, LANES), 1)
    mine = jnp.zeros((SUB, LANES), jnp.float32)
    for r in range(R):
        for base, quantity in ((0, lm), (half, mm)):
            row = jnp.sum(jnp.sum(quantity[r], axis=0), axis=0, keepdims=True)
            mine = jnp.where(sub_index == base + r, row, mine)
    mine = jnp.where((lane_index >= pad) & (lane_index < pad + wide), mine, 0.0)
    fold = LANES // 2
    while fold >= LANES // SUB:
        mine = mine + roll(mine, fold, 1)
        fold //= 2
    group = lane_index // (LANES // SUB) == sub_index
    part[...] = jnp.sum(jnp.where(group, mine, 0.0), axis=0, keepdims=True)

    def sums(side, i):
        peer = lax.rem(ax + i, n_ax)
        return pltpu.make_async_remote_copy(
            src_ref=part, dst_ref=parts.at[(1 - side) * n_ax + ax],
            send_sem=p_send.at[(1 + side) * n_ax + i], recv_sem=p_recv.at[(1 - side) * n_ax + ax],
            device_id=(peer, rad + side), device_id_type=MESH)

    def sums_in(side, i):
        peer = lax.rem(ax + i, n_ax)
        slot = (1 + side) * n_ax + peer
        return pltpu.make_async_remote_copy(
            src_ref=part, dst_ref=parts.at[slot],
            send_sem=p_send.at[(1 + side) * n_ax + i], recv_sem=p_recv.at[slot],
            device_id=(peer, rad + side), device_id_type=MESH)

    def first_of(side):
        return 1 if side == 0 else 0

    def send_sums(side):
        first = first_of(side)
        each(n_ax - first, lambda i: sums(side, i + first).start())

    send_sums(0)
    hear(len(distances) - 1)
    pl.when(has_lo)(lambda: send_sums(-1))
    pl.when(has_hi)(lambda: send_sums(1))

    for c in range(3):
        hx[c, 1 : R + 1] = stress[pair(c, 1)][:, 1:-1]

    def edge(slot, src, dst, to_rad):
        return pltpu.make_async_remote_copy(
            src_ref=hx.at[:, src], dst_ref=hx.at[:, dst], send_sem=h_send.at[slot],
            recv_sem=h_recv.at[slot], device_id=(ax, to_rad), device_id_type=MESH)

    edge_out = edge(0, R, 0, rad + 1)
    edge_in = edge(1, 1, R + 1, rad - 1)
    pl.when(has_hi)(lambda: edge_out.start())
    pl.when(has_lo)(lambda: edge_in.start())

    @pl.when(rad == 0)
    def _():
        for c in range(3):
            for z in range(Z):
                hx[c, 0, z] = SIGNS[c] * SIGNS[1] * roll(hx[c, 1, z], half, 0)

    @pl.when(rad == n_rad - 1)
    def _():
        for c in range(3):
            for z in range(Z):
                hx[c, R + 1, z] = jnp.zeros((SUB, LANES), jnp.float32)

    bases, turns = [], []
    whole = [jnp.concatenate([below[c], mids[c], above[c]], axis=0)[:, 1:-1] for c in range(3)]
    for c in range(3):
        axial = mids[c] * mids[0]
        radial = whole[c] * whole[1]
        around = whole[c][1:-1] * whole[2][1:-1]
        change = axial[:, 2:] - axial[:, :-2] + (radial[2:] - radial[:-2]) + (up(around) - down(around))
        bases.append(whole[c][1:-1] - 0.5 * change)
        along = stress[pair(c, 0)]
        turn = stress[pair(c, 2)][:, 1:-1]
        turns.append(along[:, 2:] - along[:, :-2] + (up(turn) - down(turn)))

    count = n_ax * Z * T
    each(n_ax - 1, lambda i: sums_in(0, i + 1).wait_recv())

    def coefficients(total):
        total = jnp.broadcast_to(jnp.sum(jnp.where(group, total, 0.0), axis=1, keepdims=True), (SUB, LANES)) / count
        return total / (roll(total, -half, 0) + EPSILON)

    def total_of(side):
        first = first_of(side)
        total = part[...] if first else jnp.zeros((1, LANES), jnp.float32)
        if n_ax <= 16:
            for i in range(first, n_ax):
                total = total + parts[(1 + side) * n_ax + lax.rem(ax + i, n_ax)]
            return total
        return lax.fori_loop(
            first, n_ax, lambda i, t: t + parts[(1 + side) * n_ax + lax.rem(ax + i, n_ax)], total)

    coef = coefficients(total_of(0))

    def beside(side, row):
        each(n_ax, lambda i: sums_in(side, i).wait_recv())
        edge_coef[0 if side < 0 else 1] = jnp.broadcast_to(
            coefficients(total_of(side))[row : row + 1], (SUB, LANES))

    pl.when(has_lo)(lambda: beside(-1, R - 1))
    pl.when(has_hi)(lambda: beside(1, 0))

    @pl.when(rad == 0)
    def _():
        edge_coef[0] = jnp.broadcast_to(coef[0:1], (SUB, LANES))

    @pl.when(rad == n_rad - 1)
    def _():
        edge_coef[1] = jnp.zeros((SUB, LANES), jnp.float32)

    pl.when(has_lo)(lambda: edge_out.wait_recv())
    pl.when(has_hi)(lambda: edge_in.wait_recv())
    by_row = [edge_coef[0]] + [jnp.broadcast_to(coef[r : r + 1], (SUB, LANES)) for r in range(R)] + [edge_coef[1]]
    for c in range(3):
        for r in range(R):
            new = bases[c][r] + by_row[r + 1] * turns[c][r]
            new = new + (by_row[r + 2] * hx[c, r + 2] - by_row[r] * hx[c, r])
            for z in range(Z):
                row = ((c * R + r) * Z + z) * SUB
                own[row : row + SUB, :] = new[z]
    for c in range(3):
        for r in range(R):
            for k, tile in enumerate(joined(strips(c, r), wide, pad)):
                out_ref[c, r, :, k * LANES : (k + 1) * LANES] = tile

    wait_send([z_lo, z_hi])

    @pl.when(has_hi)
    def _():
        wait_send(out_going + [edge_out])
        each(n_ax, lambda i: sums(1, i).wait_send())

    @pl.when(has_lo)
    def _():
        wait_send(in_going + [edge_in])
        each(n_ax, lambda i: sums(-1, i).wait_send())

    each(n_ax - 1, lambda i: sums(0, i + 1).wait_send())


def shards(n_ax, n_rad, velocity, cycle_map):
    _, R, Z, T = velocity.shape
    return pl.pallas_call(
        functools.partial(kernel, n_ax, n_rad),
        out_shape=jax.ShapeDtypeStruct(velocity.shape, velocity.dtype),
        in_specs=[pl.BlockSpec(memory_space=pltpu.HBM)] * 2,
        out_specs=pl.BlockSpec(memory_space=pltpu.VMEM),
        scratch_shapes=[
            pltpu.VMEM(velocity.shape, jnp.float32),
            pltpu.VMEM(cycle_map.shape, jnp.int32),
            pltpu.VMEM((3 * R * Z * SUB, LANES), jnp.float32),
            pltpu.VMEM((2 * NRING * SUB, LANES), jnp.float32),
            pltpu.VMEM((3, R + 2, Z + 4, SUB, LANES), jnp.float32),
            pltpu.VMEM((3, R + 2, Z, SUB, LANES), jnp.float32),
            pltpu.VMEM((1, LANES), jnp.float32),
            pltpu.VMEM((3 * n_ax, 1, LANES), jnp.float32),
            pltpu.VMEM((2, SUB, LANES), jnp.float32),
            pltpu.VMEM((2, 3 * R * 2 * T // LANES, LANES), jnp.float32),
            pltpu.VMEM((2, 3 * R * 2 * T // LANES, LANES), jnp.float32),
            pltpu.VMEM((2 * 3 * R * 2 * SUB, LANES), jnp.float32),
            pltpu.SemaphoreType.REGULAR((len(stages(n_ax)),)),
            pltpu.SemaphoreType.DMA((2,)),
            pltpu.SemaphoreType.DMA((8,)),
            pltpu.SemaphoreType.DMA((8,)),
            pltpu.SemaphoreType.DMA((2,)),
            pltpu.SemaphoreType.DMA((2,)),
            pltpu.SemaphoreType.DMA((3 * n_ax,)),
            pltpu.SemaphoreType.DMA((3 * n_ax,)),
        ],
        compiler_params=pltpu.CompilerParams(collective_id=0, has_side_effects=True, vmem_limit_bytes=8 << 20),
    )(*(pltpu.with_memory_space_constraint(x, pltpu.HBM) for x in (velocity, cycle_map)))


def solution(mesh):
    n_ax, n_rad = mesh.shape["ax"], mesh.shape["rad"]
    spec = P(None, "rad", "ax", None)
    body = functools.partial(shards, n_ax, n_rad)
    return jax.shard_map(body, mesh=mesh, in_specs=(spec, P()), out_specs=spec, check_vma=False)
```

```python
import functools

import jax
import jax.numpy as jnp
from jax import lax
from jax.experimental import pallas as pl
from jax.experimental.pallas import tpu as pltpu
from jax.sharding import PartitionSpec as P

NRING = 3
MOSTSEG = 16
SUB = 8
LANES = 128
PAIRS = ((0, 0), (1, 1), (2, 2), (0, 1), (0, 2), (1, 2))
PAIR_WEIGHTS = (1.0, 1.0, 1.0, 2.0, 2.0, 2.0)
SIGNS = (1.0, -1.0, -1.0)
EPSILON = 1e-06
MESH = pl.DeviceIdType.MESH


def pair(a, b):
    return PAIRS.index((min(a, b), max(a, b)))


def each(count, body):
    if count <= 16:
        for i in range(count):
            body(i)
    else:
        lax.fori_loop(0, count, lambda i, c: (body(i), c)[1], 0)


def roll(x, shift, axis):
    size = x.shape[axis]
    return pltpu.roll(x, shift % size, axis)


def up(x):
    return roll(x, -1, x.ndim - 1)


def down(x):
    return roll(x, 1, x.ndim - 1)


def smooth_t(x):
    return (down(x) + 2.0 * x + up(x)) * 0.25


def smooth_z(x):
    return (x[:, :-2] + 2.0 * x[:, 1:-1] + x[:, 2:]) * 0.25


def tiles_of(x):
    return [x[:, k : k + LANES] for k in range(0, x.shape[1], LANES)]


def segments(x, wide, pad):
    rows, tiles = x[0].shape[0], len(x)
    total = tiles * LANES
    lane = lax.broadcasted_iota(jnp.int32, (rows, LANES), 1)
    pieces = []
    for s in range(SUB):
        start = (s * wide - pad) % total
        k, off = start // LANES, start % LANES
        first = x[k]
        if off:
            k2 = (k + 1) % tiles
            second = x[k2]
            first = jnp.where(lane < LANES - off, roll(first, -off, 1), roll(second, -off, 1))
        pieces.append(first)
    return pieces


def joined(pieces, wide, pad):
    rows = pieces[0].shape[0]
    lane = lax.broadcasted_iota(jnp.int32, (rows, LANES), 1)
    tiles = []
    for k in range(SUB * wide // LANES):
        lo, hi = k * LANES, (k + 1) * LANES
        s = lo // wide
        out = None
        while s * wide < hi:
            part = roll(pieces[s], s * wide - pad - lo, 1)
            out = part if out is None else jnp.where(lane >= s * wide - lo, part, out)
            s += 1
        tiles.append(out)
    return tiles


def strain(grads):
    tensor = []
    for c, a in PAIRS:
        if c == a:
            tensor.append(0.5 * grads[c][c])
        else:
            tensor.append(0.25 * (grads[c][a] + grads[a][c]))
    squares = sum(w * m * m for w, m in zip(PAIR_WEIGHTS, tensor))
    return tensor, jnp.sqrt(2.0 * squares)


def gradients(f):
    out = []
    for c in range(3):
        mid = f[c][1:-1, 1:-1]
        out.append(
            [
                f[c][1:-1, 2:] - f[c][1:-1, :-2],
                f[c][2:, 1:-1] - f[c][:-2, 1:-1],
                up(mid) - down(mid),
            ]
        )
    return out


def stages(n_ax):
    distances, own, beside = [1], 2, 1
    while own < n_ax // 2:
        distances.append(own)
        own, beside = 2 * own, beside + own
    while beside < n_ax // 2:
        distances.append(1)
        beside += 1
    return distances


def kernel(n_ax, n_rad, v_hbm, map_hbm, out_ref, nat, map_ref, own, maps, ext, hx, part, parts, edge_coef,
           z_out, z_in, z_seg, ready, in_sems, halo_send, halo_recv, h_send, h_recv, p_send, p_recv):
    rad = lax.axis_index("rad")
    ax = lax.axis_index("ax")
    R, Z, T = nat.shape[1], nat.shape[2], nat.shape[3]
    wide = T // SUB
    pad = (LANES - wide) // 2
    half = SUB // 2
    right, left = lax.rem(ax + 1, n_ax), lax.rem(ax + n_ax - 1, n_ax)
    has_lo, has_hi = rad > 0, rad < n_rad - 1

    def strips(c, r):
        return [own[pl.ds((c * R + r) * Z * SUB + s, Z, stride=SUB), :] for s in range(SUB)]

    barrier = pltpu.get_barrier_semaphore()

    def greet(to_ax, to_rad):
        pl.semaphore_signal(barrier, inc=1, device_id=(to_ax, to_rad), device_id_type=MESH)

    greet(left, rad)
    greet(right, rad)
    pl.when(has_lo)(lambda: greet(ax, rad - 1))
    pl.when(has_hi)(lambda: greet(ax, rad + 1))

    distances = stages(n_ax)

    def tell(stage):
        d = distances[stage]
        for peer in (lax.rem(ax + d, n_ax), lax.rem(ax + n_ax - d, n_ax)):
            pl.semaphore_signal(ready.at[stage], inc=1, device_id=(peer, rad), device_id_type=MESH)

    def hear(stage):
        pl.semaphore_wait(ready.at[stage], 2)

    fetch = pltpu.make_async_copy(v_hbm, nat, in_sems.at[0])
    fetch.start()
    fetch_map = pltpu.make_async_copy(map_hbm, map_ref, in_sems.at[1])
    pl.when(rad == 0)(lambda: fetch_map.start())
    fetch.wait()
    for c in range(3):
        for r in range(R):
            for s, piece in enumerate(segments(tiles_of(nat[c, r]), wide, pad)):
                own[pl.ds((c * R + r) * Z * SUB + s, Z, stride=SUB), :] = piece
    for c in range(3):
        for r in range(R):
            for z in range(Z):
                row = ((c * R + r) * Z + z) * SUB
                ext[c, r + 1, z + 2] = own[row : row + SUB, :]

    lane = lax.broadcasted_iota(jnp.int32, (SUB, LANES), 1)
    steps = []
    while 2 ** len(steps) < MOSTSEG:
        steps.append(2 ** len(steps))

    def cell_sums(r):
        label = maps[r * SUB : (r + 1) * SUB, :]
        before = [(roll(label, d, 1) == label).astype(jnp.float32) for d in steps]
        after = [(roll(label, -d, 1) == label).astype(jnp.float32) for d in steps]

        def spread(x):
            total, rest = x, x
            for d, b, a in zip(steps, before, after):
                total = total + b * roll(total, d, 1)
                rest = rest + a * roll(rest, -d, 1)
            return total + rest - x

        return spread

    def coarsen(r, spread, c, z):
        mean = spread(ext[c, r + 1, z]) * maps[(NRING + r) * SUB : (NRING + r + 1) * SUB, :]
        low = roll(roll(mean, -wide, 1), 1, 0)
        high = roll(roll(mean, wide, 1), -1, 0)
        mean = jnp.where(lane < pad, low, mean)
        ext[c, r + 1, z] = jnp.where(lane >= pad + wide, high, mean)

    @pl.when(rad == 0)
    def _():
        fetch_map.wait()
        labels = map_ref[...].astype(jnp.float32)
        for s, piece in enumerate(segments(tiles_of(labels), wide, pad)):
            maps[pl.ds(s, NRING, stride=SUB), :] = piece
        for r in range(NRING):
            spread = cell_sums(r)
            maps[(NRING + r) * SUB : (NRING + r + 1) * SUB, :] = 1.0 / spread(jnp.ones((SUB, LANES), jnp.float32))
            for c in range(3):
                for z in range(Z):
                    coarsen(r, spread, c, z + 2)
                    row = ((c * R + r) * Z + z) * SUB
                    own[row : row + SUB, :] = ext[c, r + 1, z + 2]
                for k, tile in enumerate(joined(strips(c, r), wide, pad)):
                    nat[c, r, :, k * LANES : (k + 1) * LANES] = tile

    n_rows = 3 * R * 2
    for side, first in ((0, Z - 2), (1, 0)):
        for c in range(3):
            for r in range(R):
                for k in range(T // LANES):
                    row = k * n_rows + (c * R + r) * 2
                    z_out[side, row : row + 2, :] = nat[c, r, first : first + 2, k * LANES : (k + 1) * LANES]

    pl.semaphore_wait(barrier, 2 + jnp.where(has_lo, 1, 0) + jnp.where(has_hi, 1, 0))

    def z_halo(slot, to_ax):
        return pltpu.make_async_remote_copy(
            src_ref=z_out.at[slot], dst_ref=z_in.at[slot], send_sem=halo_send.at[slot],
            recv_sem=halo_recv.at[slot], device_id=(to_ax, rad), device_id_type=MESH)

    z_lo, z_hi = z_halo(0, right), z_halo(1, left)
    z_lo.start()
    z_hi.start()
    tell(0)

    rows, cols = pl.ds(1, R), pl.ds(2, Z)

    def halo(slot, src, dst, to_ax, to_rad):
        return pltpu.make_async_remote_copy(
            src_ref=ext.at[src], dst_ref=ext.at[dst], send_sem=halo_send.at[slot],
            recv_sem=halo_recv.at[slot], device_id=(to_ax, to_rad), device_id_type=MESH)

    everything = slice(None)

    out_going = [
        halo(2, (everything, R, cols), (everything, 0, cols), ax, rad + 1),
        halo(3, (everything, R, Z + 1), (everything, 0, 1), right, rad + 1),
        halo(4, (everything, R, 2), (everything, 0, Z + 2), left, rad + 1),
    ]
    in_going = [
        halo(5, (everything, 1, cols), (everything, R + 1, cols), ax, rad - 1),
        halo(6, (everything, 1, Z + 1), (everything, R + 1, 1), right, rad - 1),
        halo(7, (everything, 1, 2), (everything, R + 1, Z + 2), left, rad - 1),
    ]

    def start_all(copies):
        for copy in copies:
            copy.start()

    def wait_recv(copies):
        for copy in copies:
            copy.wait_recv()

    def wait_send(copies):
        for copy in copies:
            copy.wait_send()

    pl.when(has_hi)(lambda: start_all(out_going[:1]))
    pl.when(has_lo)(lambda: start_all(in_going[:1]))
    for stage in range(len(distances) - 1)[:1]:
        hear(stage)
        tell(stage + 1)
    pl.when(has_hi)(lambda: start_all(out_going[1:]))
    pl.when(has_lo)(lambda: start_all(in_going[1:]))
    for side, copy, first in ((0, z_lo, 0), (1, z_hi, Z + 2)):
        copy.wait_recv()
        tiles = [z_in[side, k * n_rows : (k + 1) * n_rows, :] for k in range(T // LANES)]
        for s, piece in enumerate(segments(tiles, wide, pad)):
            z_seg[pl.ds(side * n_rows * SUB + s, n_rows, stride=SUB), :] = piece
        for c in range(3):
            for r in range(R):
                for z in range(2):
                    row = (side * n_rows + (c * R + r) * 2 + z) * SUB
                    ext[c, r + 1, first + z] = z_seg[row : row + SUB, :]
    for stage in range(1, len(distances) - 1):
        hear(stage)
        tell(stage + 1)

    long = [ext[c, 1 : R + 1, 0 : Z + 4] for c in range(3)]
    mids = [x[:, 1:-1] for x in long]
    grads, w_own, w_grads, leonards = [], [], [], []
    for c in range(3):
        turned = up(mids[c]) - down(mids[c])
        grads.append([long[c][:, 2:] - long[c][:, :-2], None, turned])
        w_own.append(smooth_t(smooth_z(long[c])))
        mid = w_own[c][:, 1:-1]
        w_grads.append([w_own[c][:, 2:] - w_own[c][:, :-2], None, up(mid) - down(mid)])
    for c, a in PAIRS:
        product = smooth_t(smooth_z(mids[c] * mids[a]))
        leonards.append(product - w_own[c][:, 1:-1] * w_own[a][:, 1:-1])

    pl.when(has_lo)(lambda: wait_recv(out_going))
    pl.when(has_hi)(lambda: wait_recv(in_going))

    @pl.when(rad == 0)
    def _():
        for c in range(3):
            for z in range(1, Z + 3):
                ext[c, 0, z] = SIGNS[c] * roll(ext[c, 1, z], half, 0)

    @pl.when(rad == n_rad - 1)
    def _():
        for c in range(3):
            for z in range(1, Z + 3):
                ext[c, R + 1, z] = jnp.zeros((SUB, LANES), jnp.float32)

    below = [ext[c, 0:1, 1 : Z + 3] for c in range(3)]
    above = [ext[c, R + 1 : R + 2, 1 : Z + 3] for c in range(3)]
    for c in range(3):
        column = jnp.concatenate([below[c], mids[c], above[c]], axis=0)
        grads[c][1] = column[2:] - column[:-2]
        column = jnp.concatenate(
            [smooth_t(smooth_z(below[c])), w_own[c][:, 1:-1], smooth_t(smooth_z(above[c]))], axis=0)
        w_grads[c][1] = column[2:] - column[:-2]
    tensor, mag = strain(grads)
    stress = [mag * t for t in tensor]
    w_tensor, w_mag = strain(w_grads)
    w_mag4 = 4.0 * w_mag
    lm, mm = 0.0, 0.0
    for number, leonard in enumerate(leonards):
        model = smooth_t(smooth_z(stress[number])) - w_mag4 * w_tensor[number]
        lm = lm + PAIR_WEIGHTS[number] * leonard * model
        mm = mm + PAIR_WEIGHTS[number] * model * model
    sub_index = lax.broadcasted_iota(jnp.int32, (SUB, LANES), 0)
    lane_index = lax.broadcasted_iota(jnp.int32, (SUB, LANES), 1)
    mine = jnp.zeros((SUB, LANES), jnp.float32)
    for r in range(R):
        for base, quantity in ((0, lm), (half, mm)):
            row = jnp.sum(jnp.sum(quantity[r], axis=0), axis=0, keepdims=True)
            mine = jnp.where(sub_index == base + r, row, mine)
    mine = jnp.where((lane_index >= pad) & (lane_index < pad + wide), mine, 0.0)
    fold = LANES // 2
    while fold >= LANES // SUB:
        mine = mine + roll(mine, fold, 1)
        fold //= 2
    group = lane_index // (LANES // SUB) == sub_index
    part[...] = jnp.sum(jnp.where(group, mine, 0.0), axis=0, keepdims=True)

    def sums(side, i):
        peer = lax.rem(ax + i, n_ax)
        return pltpu.make_async_remote_copy(
            src_ref=part, dst_ref=parts.at[(1 - side) * n_ax + ax],
            send_sem=p_send.at[(1 + side) * n_ax + i], recv_sem=p_recv.at[(1 - side) * n_ax + ax],
            device_id=(peer, rad + side), device_id_type=MESH)

    def sums_in(side, i):
        peer = lax.rem(ax + i, n_ax)
        slot = (1 + side) * n_ax + peer
        return pltpu.make_async_remote_copy(
            src_ref=part, dst_ref=parts.at[slot],
            send_sem=p_send.at[(1 + side) * n_ax + i], recv_sem=p_recv.at[slot],
            device_id=(peer, rad + side), device_id_type=MESH)

    def first_of(side):
        return 1 if side == 0 else 0

    def send_sums(side):
        first = first_of(side)
        each(n_ax - first, lambda i: sums(side, i + first).start())

    send_sums(0)
    hear(len(distances) - 1)
    pl.when(has_lo)(lambda: send_sums(-1))
    pl.when(has_hi)(lambda: send_sums(1))

    for c in range(3):
        hx[c, 1 : R + 1] = stress[pair(c, 1)][:, 1:-1]

    def edge(slot, src, dst, to_rad):
        return pltpu.make_async_remote_copy(
            src_ref=hx.at[:, src], dst_ref=hx.at[:, dst], send_sem=h_send.at[slot],
            recv_sem=h_recv.at[slot], device_id=(ax, to_rad), device_id_type=MESH)

    edge_out = edge(0, R, 0, rad + 1)
    edge_in = edge(1, 1, R + 1, rad - 1)
    pl.when(has_hi)(lambda: edge_out.start())
    pl.when(has_lo)(lambda: edge_in.start())

    @pl.when(rad == 0)
    def _():
        for c in range(3):
            for z in range(Z):
                hx[c, 0, z] = SIGNS[c] * SIGNS[1] * roll(hx[c, 1, z], half, 0)

    @pl.when(rad == n_rad - 1)
    def _():
        for c in range(3):
            for z in range(Z):
                hx[c, R + 1, z] = jnp.zeros((SUB, LANES), jnp.float32)

    bases, turns = [], []
    whole = [jnp.concatenate([below[c], mids[c], above[c]], axis=0)[:, 1:-1] for c in range(3)]
    for c in range(3):
        axial = mids[c] * mids[0]
        radial = whole[c] * whole[1]
        around = whole[c][1:-1] * whole[2][1:-1]
        change = axial[:, 2:] - axial[:, :-2] + (radial[2:] - radial[:-2]) + (up(around) - down(around))
        bases.append(whole[c][1:-1] - 0.5 * change)
        along = stress[pair(c, 0)]
        turn = stress[pair(c, 2)][:, 1:-1]
        turns.append(along[:, 2:] - along[:, :-2] + (up(turn) - down(turn)))

    count = n_ax * Z * T
    each(n_ax - 1, lambda i: sums_in(0, i + 1).wait_recv())

    def coefficients(total):
        total = jnp.broadcast_to(jnp.sum(jnp.where(group, total, 0.0), axis=1, keepdims=True), (SUB, LANES)) / count
        return total / (roll(total, -half, 0) + EPSILON)

    def total_of(side):
        first = first_of(side)
        total = part[...] if first else jnp.zeros((1, LANES), jnp.float32)
        if n_ax <= 16:
            for i in range(first, n_ax):
                total = total + parts[(1 + side) * n_ax + lax.rem(ax + i, n_ax)]
            return total
        return lax.fori_loop(
            first, n_ax, lambda i, t: t + parts[(1 + side) * n_ax + lax.rem(ax + i, n_ax)], total)

    coef = coefficients(total_of(0))

    def beside(side, row):
        each(n_ax, lambda i: sums_in(side, i).wait_recv())
        edge_coef[0 if side < 0 else 1] = jnp.broadcast_to(
            coefficients(total_of(side))[row : row + 1], (SUB, LANES))

    pl.when(has_lo)(lambda: beside(-1, R - 1))
    pl.when(has_hi)(lambda: beside(1, 0))

    @pl.when(rad == 0)
    def _():
        edge_coef[0] = jnp.broadcast_to(coef[0:1], (SUB, LANES))

    @pl.when(rad == n_rad - 1)
    def _():
        edge_coef[1] = jnp.zeros((SUB, LANES), jnp.float32)

    pl.when(has_lo)(lambda: edge_out.wait_recv())
    pl.when(has_hi)(lambda: edge_in.wait_recv())
    by_row = [edge_coef[0]] + [jnp.broadcast_to(coef[r : r + 1], (SUB, LANES)) for r in range(R)] + [edge_coef[1]]
    for c in range(3):
        for r in range(R):
            new = bases[c][r] + by_row[r + 1] * turns[c][r]
            new = new + (by_row[r + 2] * hx[c, r + 2] - by_row[r] * hx[c, r])
            for z in range(Z):
                row = ((c * R + r) * Z + z) * SUB
                own[row : row + SUB, :] = new[z]
    for c in range(3):
        for r in range(R):
            for k, tile in enumerate(joined(strips(c, r), wide, pad)):
                out_ref[c, r, :, k * LANES : (k + 1) * LANES] = tile

    wait_send([z_lo, z_hi])

    @pl.when(has_hi)
    def _():
        wait_send(out_going + [edge_out])
        each(n_ax, lambda i: sums(1, i).wait_send())

    @pl.when(has_lo)
    def _():
        wait_send(in_going + [edge_in])
        each(n_ax, lambda i: sums(-1, i).wait_send())

    each(n_ax - 1, lambda i: sums(0, i + 1).wait_send())


def shards(n_ax, n_rad, velocity, cycle_map):
    _, R, Z, T = velocity.shape
    return pl.pallas_call(
        functools.partial(kernel, n_ax, n_rad),
        out_shape=jax.ShapeDtypeStruct(velocity.shape, velocity.dtype),
        in_specs=[pl.BlockSpec(memory_space=pltpu.HBM)] * 2,
        out_specs=pl.BlockSpec(memory_space=pltpu.VMEM),
        scratch_shapes=[
            pltpu.VMEM(velocity.shape, jnp.float32),
            pltpu.VMEM(cycle_map.shape, jnp.int32),
            pltpu.VMEM((3 * R * Z * SUB, LANES), jnp.float32),
            pltpu.VMEM((2 * NRING * SUB, LANES), jnp.float32),
            pltpu.VMEM((3, R + 2, Z + 4, SUB, LANES), jnp.float32),
            pltpu.VMEM((3, R + 2, Z, SUB, LANES), jnp.float32),
            pltpu.VMEM((1, LANES), jnp.float32),
            pltpu.VMEM((3 * n_ax, 1, LANES), jnp.float32),
            pltpu.VMEM((2, SUB, LANES), jnp.float32),
            pltpu.VMEM((2, 3 * R * 2 * T // LANES, LANES), jnp.float32),
            pltpu.VMEM((2, 3 * R * 2 * T // LANES, LANES), jnp.float32),
            pltpu.VMEM((2 * 3 * R * 2 * SUB, LANES), jnp.float32),
            pltpu.SemaphoreType.REGULAR((len(stages(n_ax)),)),
            pltpu.SemaphoreType.DMA((2,)),
            pltpu.SemaphoreType.DMA((8,)),
            pltpu.SemaphoreType.DMA((8,)),
            pltpu.SemaphoreType.DMA((2,)),
            pltpu.SemaphoreType.DMA((2,)),
            pltpu.SemaphoreType.DMA((3 * n_ax,)),
            pltpu.SemaphoreType.DMA((3 * n_ax,)),
        ],
        compiler_params=pltpu.CompilerParams(collective_id=0, has_side_effects=True, vmem_limit_bytes=8 << 20),
    )(*(pltpu.with_memory_space_constraint(x, pltpu.HBM) for x in (velocity, cycle_map)))


def solution(mesh):
    n_ax, n_rad = mesh.shape["ax"], mesh.shape["rad"]
    spec = P(None, "rad", "ax", None)
    body = functools.partial(shards, n_ax, n_rad)
    return jax.shard_map(body, mesh=mesh, in_specs=(spec, P()), out_specs=spec, check_vma=False)
```

```python
import functools

import jax
import jax.numpy as jnp
from jax import lax
from jax.experimental import pallas as pl
from jax.experimental.pallas import tpu as pltpu
from jax.sharding import PartitionSpec as P

NRING = 3
MOSTSEG = 16
SUB = 8
LANES = 128
PAIRS = ((0, 0), (1, 1), (2, 2), (0, 1), (0, 2), (1, 2))
PAIR_WEIGHTS = (1.0, 1.0, 1.0, 2.0, 2.0, 2.0)
SIGNS = (1.0, -1.0, -1.0)
EPSILON = 1e-06
MESH = pl.DeviceIdType.MESH


def pair(a, b):
    return PAIRS.index((min(a, b), max(a, b)))


def each(count, body):
    if count <= 16:
        for i in range(count):
            body(i)
    else:
        lax.fori_loop(0, count, lambda i, c: (body(i), c)[1], 0)


def roll(x, shift, axis):
    size = x.shape[axis]
    return pltpu.roll(x, shift % size, axis)


def up(x):
    return roll(x, -1, x.ndim - 1)


def down(x):
    return roll(x, 1, x.ndim - 1)


def smooth_t(x):
    return (down(x) + 2.0 * x + up(x)) * 0.25


def smooth_z(x):
    return (x[:, :-2] + 2.0 * x[:, 1:-1] + x[:, 2:]) * 0.25


def tiles_of(x):
    return [x[:, k : k + LANES] for k in range(0, x.shape[1], LANES)]


def segments(x, wide, pad):
    rows, tiles = x[0].shape[0], len(x)
    total = tiles * LANES
    lane = lax.broadcasted_iota(jnp.int32, (rows, LANES), 1)
    pieces = []
    for s in range(SUB):
        start = (s * wide - pad) % total
        k, off = start // LANES, start % LANES
        first = x[k]
        if off:
            k2 = (k + 1) % tiles
            second = x[k2]
            first = jnp.where(lane < LANES - off, roll(first, -off, 1), roll(second, -off, 1))
        pieces.append(first)
    return pieces


def joined(pieces, wide, pad):
    rows = pieces[0].shape[0]
    lane = lax.broadcasted_iota(jnp.int32, (rows, LANES), 1)
    tiles = []
    for k in range(SUB * wide // LANES):
        lo, hi = k * LANES, (k + 1) * LANES
        s = lo // wide
        out = None
        while s * wide < hi:
            part = roll(pieces[s], s * wide - pad - lo, 1)
            out = part if out is None else jnp.where(lane >= s * wide - lo, part, out)
            s += 1
        tiles.append(out)
    return tiles


def strain(grads):
    tensor = []
    for c, a in PAIRS:
        if c == a:
            tensor.append(0.5 * grads[c][c])
        else:
            tensor.append(0.25 * (grads[c][a] + grads[a][c]))
    squares = sum(w * m * m for w, m in zip(PAIR_WEIGHTS, tensor))
    return tensor, jnp.sqrt(2.0 * squares)


def gradients(f):
    out = []
    for c in range(3):
        mid = f[c][1:-1, 1:-1]
        out.append(
            [
                f[c][1:-1, 2:] - f[c][1:-1, :-2],
                f[c][2:, 1:-1] - f[c][:-2, 1:-1],
                up(mid) - down(mid),
            ]
        )
    return out


def stages(n_ax):
    distances, own, beside = [1], 2, 1
    while own < n_ax // 2:
        distances.append(own)
        own, beside = 2 * own, beside + own
    while beside < n_ax // 2:
        distances.append(1)
        beside += 1
    return distances


def kernel(n_ax, n_rad, v_hbm, map_hbm, out_ref, nat, map_ref, own, maps, ext, hx, part, parts, edge_coef,
           z_out, z_in, z_seg, ready, in_sems, halo_send, halo_recv, h_send, h_recv, p_send, p_recv):
    rad = lax.axis_index("rad")
    ax = lax.axis_index("ax")
    R, Z, T = nat.shape[1], nat.shape[2], nat.shape[3]
    wide = T // SUB
    pad = (LANES - wide) // 2
    half = SUB // 2
    right, left = lax.rem(ax + 1, n_ax), lax.rem(ax + n_ax - 1, n_ax)
    has_lo, has_hi = rad > 0, rad < n_rad - 1

    def strips(c, r):
        return [own[pl.ds((c * R + r) * Z * SUB + s, Z, stride=SUB), :] for s in range(SUB)]

    barrier = pltpu.get_barrier_semaphore()

    def greet(to_ax, to_rad):
        pl.semaphore_signal(barrier, inc=1, device_id=(to_ax, to_rad), device_id_type=MESH)

    greet(left, rad)
    greet(right, rad)
    pl.when(has_lo)(lambda: greet(ax, rad - 1))
    pl.when(has_hi)(lambda: greet(ax, rad + 1))

    distances = stages(n_ax)

    def tell(stage):
        d = distances[stage]
        for peer in (lax.rem(ax + d, n_ax), lax.rem(ax + n_ax - d, n_ax)):
            pl.semaphore_signal(ready.at[stage], inc=1, device_id=(peer, rad), device_id_type=MESH)

    def hear(stage):
        pl.semaphore_wait(ready.at[stage], 2)

    fetch = pltpu.make_async_copy(v_hbm, nat, in_sems.at[0])
    fetch.start()
    fetch_map = pltpu.make_async_copy(map_hbm, map_ref, in_sems.at[1])
    pl.when(rad == 0)(lambda: fetch_map.start())
    fetch.wait()
    for c in range(3):
        for r in range(R):
            for s, piece in enumerate(segments(tiles_of(nat[c, r]), wide, pad)):
                own[pl.ds((c * R + r) * Z * SUB + s, Z, stride=SUB), :] = piece
    for c in range(3):
        for r in range(R):
            for z in range(Z):
                row = ((c * R + r) * Z + z) * SUB
                ext[c, r + 1, z + 2] = own[row : row + SUB, :]

    lane = lax.broadcasted_iota(jnp.int32, (SUB, LANES), 1)
    steps = []
    while 2 ** len(steps) < MOSTSEG:
        steps.append(2 ** len(steps))

    def cell_sums(r):
        label = maps[r * SUB : (r + 1) * SUB, :]
        before = [(roll(label, d, 1) == label).astype(jnp.float32) for d in steps]
        after = [(roll(label, -d, 1) == label).astype(jnp.float32) for d in steps]

        def spread(x):
            total, rest = x, x
            for d, b, a in zip(steps, before, after):
                total = total + b * roll(total, d, 1)
                rest = rest + a * roll(rest, -d, 1)
            return total + rest - x

        return spread

    def coarsen(r, spread, c, z):
        mean = spread(ext[c, r + 1, z]) * maps[(NRING + r) * SUB : (NRING + r + 1) * SUB, :]
        low = roll(roll(mean, -wide, 1), 1, 0)
        high = roll(roll(mean, wide, 1), -1, 0)
        mean = jnp.where(lane < pad, low, mean)
        ext[c, r + 1, z] = jnp.where(lane >= pad + wide, high, mean)

    @pl.when(rad == 0)
    def _():
        fetch_map.wait()
        labels = map_ref[...].astype(jnp.float32)
        for s, piece in enumerate(segments(tiles_of(labels), wide, pad)):
            maps[pl.ds(s, NRING, stride=SUB), :] = piece
        for r in range(NRING):
            spread = cell_sums(r)
            maps[(NRING + r) * SUB : (NRING + r + 1) * SUB, :] = 1.0 / spread(jnp.ones((SUB, LANES), jnp.float32))
            for c in range(3):
                for z in range(Z):
                    coarsen(r, spread, c, z + 2)
                    row = ((c * R + r) * Z + z) * SUB
                    own[row : row + SUB, :] = ext[c, r + 1, z + 2]
                for k, tile in enumerate(joined(strips(c, r), wide, pad)):
                    nat[c, r, :, k * LANES : (k + 1) * LANES] = tile

    n_rows = 3 * R * 2
    for side, first in ((0, Z - 2), (1, 0)):
        for c in range(3):
            for r in range(R):
                for k in range(T // LANES):
                    row = k * n_rows + (c * R + r) * 2
                    z_out[side, row : row + 2, :] = nat[c, r, first : first + 2, k * LANES : (k + 1) * LANES]

    pl.semaphore_wait(barrier, 2 + jnp.where(has_lo, 1, 0) + jnp.where(has_hi, 1, 0))

    def z_halo(slot, to_ax):
        return pltpu.make_async_remote_copy(
            src_ref=z_out.at[slot], dst_ref=z_in.at[slot], send_sem=halo_send.at[slot],
            recv_sem=halo_recv.at[slot], device_id=(to_ax, rad), device_id_type=MESH)

    z_lo, z_hi = z_halo(0, right), z_halo(1, left)
    z_lo.start()
    z_hi.start()
    tell(0)

    rows, cols = pl.ds(1, R), pl.ds(2, Z)

    def halo(slot, src, dst, to_ax, to_rad):
        return pltpu.make_async_remote_copy(
            src_ref=ext.at[src], dst_ref=ext.at[dst], send_sem=halo_send.at[slot],
            recv_sem=halo_recv.at[slot], device_id=(to_ax, to_rad), device_id_type=MESH)

    everything = slice(None)

    out_going = [
        halo(2, (everything, R, cols), (everything, 0, cols), ax, rad + 1),
        halo(3, (everything, R, 1), (everything, 0, 1), ax, rad + 1),
        halo(4, (everything, R, Z + 2), (everything, 0, Z + 2), ax, rad + 1),
    ]
    in_going = [
        halo(5, (everything, 1, cols), (everything, R + 1, cols), ax, rad - 1),
        halo(6, (everything, 1, 1), (everything, R + 1, 1), ax, rad - 1),
        halo(7, (everything, 1, Z + 2), (everything, R + 1, Z + 2), ax, rad - 1),
    ]

    def start_all(copies):
        for copy in copies:
            copy.start()

    def wait_recv(copies):
        for copy in copies:
            copy.wait_recv()

    def wait_send(copies):
        for copy in copies:
            copy.wait_send()

    pl.when(has_hi)(lambda: start_all(out_going[:1]))
    pl.when(has_lo)(lambda: start_all(in_going[:1]))
    for stage in range(len(distances) - 1)[:1]:
        hear(stage)
        tell(stage + 1)
    for side, copy, first in ((0, z_lo, 0), (1, z_hi, Z + 2)):
        copy.wait_recv()
        tiles = [z_in[side, k * n_rows : (k + 1) * n_rows, :] for k in range(T // LANES)]
        for s, piece in enumerate(segments(tiles, wide, pad)):
            z_seg[pl.ds(side * n_rows * SUB + s, n_rows, stride=SUB), :] = piece
        for c in range(3):
            for r in range(R):
                for z in range(2):
                    row = (side * n_rows + (c * R + r) * 2 + z) * SUB
                    ext[c, r + 1, first + z] = z_seg[row : row + SUB, :]
    pl.when(has_hi)(lambda: start_all(out_going[1:]))
    pl.when(has_lo)(lambda: start_all(in_going[1:]))
    for stage in range(1, len(distances) - 1):
        hear(stage)
        tell(stage + 1)

    long = [ext[c, 1 : R + 1, 0 : Z + 4] for c in range(3)]
    mids = [x[:, 1:-1] for x in long]
    grads, w_own, w_grads, leonards = [], [], [], []
    for c in range(3):
        turned = up(mids[c]) - down(mids[c])
        grads.append([long[c][:, 2:] - long[c][:, :-2], None, turned])
        w_own.append(smooth_t(smooth_z(long[c])))
        mid = w_own[c][:, 1:-1]
        w_grads.append([w_own[c][:, 2:] - w_own[c][:, :-2], None, up(mid) - down(mid)])
    for c, a in PAIRS:
        product = smooth_t(smooth_z(mids[c] * mids[a]))
        leonards.append(product - w_own[c][:, 1:-1] * w_own[a][:, 1:-1])

    pl.when(has_lo)(lambda: wait_recv(out_going))
    pl.when(has_hi)(lambda: wait_recv(in_going))

    @pl.when(rad == 0)
    def _():
        for c in range(3):
            for z in range(1, Z + 3):
                ext[c, 0, z] = SIGNS[c] * roll(ext[c, 1, z], half, 0)

    @pl.when(rad == n_rad - 1)
    def _():
        for c in range(3):
            for z in range(1, Z + 3):
                ext[c, R + 1, z] = jnp.zeros((SUB, LANES), jnp.float32)

    below = [ext[c, 0:1, 1 : Z + 3] for c in range(3)]
    above = [ext[c, R + 1 : R + 2, 1 : Z + 3] for c in range(3)]
    for c in range(3):
        column = jnp.concatenate([below[c], mids[c], above[c]], axis=0)
        grads[c][1] = column[2:] - column[:-2]
        column = jnp.concatenate(
            [smooth_t(smooth_z(below[c])), w_own[c][:, 1:-1], smooth_t(smooth_z(above[c]))], axis=0)
        w_grads[c][1] = column[2:] - column[:-2]
    tensor, mag = strain(grads)
    stress = [mag * t for t in tensor]
    w_tensor, w_mag = strain(w_grads)
    w_mag4 = 4.0 * w_mag
    lm, mm = 0.0, 0.0
    for number, leonard in enumerate(leonards):
        model = smooth_t(smooth_z(stress[number])) - w_mag4 * w_tensor[number]
        lm = lm + PAIR_WEIGHTS[number] * leonard * model
        mm = mm + PAIR_WEIGHTS[number] * model * model
    sub_index = lax.broadcasted_iota(jnp.int32, (SUB, LANES), 0)
    lane_index = lax.broadcasted_iota(jnp.int32, (SUB, LANES), 1)
    mine = jnp.zeros((SUB, LANES), jnp.float32)
    for r in range(R):
        for base, quantity in ((0, lm), (half, mm)):
            row = jnp.sum(jnp.sum(quantity[r], axis=0), axis=0, keepdims=True)
            mine = jnp.where(sub_index == base + r, row, mine)
    mine = jnp.where((lane_index >= pad) & (lane_index < pad + wide), mine, 0.0)
    fold = LANES // 2
    while fold >= LANES // SUB:
        mine = mine + roll(mine, fold, 1)
        fold //= 2
    group = lane_index // (LANES // SUB) == sub_index
    part[...] = jnp.sum(jnp.where(group, mine, 0.0), axis=0, keepdims=True)

    def sums(side, i):
        peer = lax.rem(ax + i, n_ax)
        return pltpu.make_async_remote_copy(
            src_ref=part, dst_ref=parts.at[(1 - side) * n_ax + ax],
            send_sem=p_send.at[(1 + side) * n_ax + i], recv_sem=p_recv.at[(1 - side) * n_ax + ax],
            device_id=(peer, rad + side), device_id_type=MESH)

    def sums_in(side, i):
        peer = lax.rem(ax + i, n_ax)
        slot = (1 + side) * n_ax + peer
        return pltpu.make_async_remote_copy(
            src_ref=part, dst_ref=parts.at[slot],
            send_sem=p_send.at[(1 + side) * n_ax + i], recv_sem=p_recv.at[slot],
            device_id=(peer, rad + side), device_id_type=MESH)

    def first_of(side):
        return 1 if side == 0 else 0

    def send_sums(side):
        first = first_of(side)
        each(n_ax - first, lambda i: sums(side, i + first).start())

    send_sums(0)
    hear(len(distances) - 1)
    pl.when(has_lo)(lambda: send_sums(-1))
    pl.when(has_hi)(lambda: send_sums(1))

    for c in range(3):
        hx[c, 1 : R + 1] = stress[pair(c, 1)][:, 1:-1]

    def edge(slot, src, dst, to_rad):
        return pltpu.make_async_remote_copy(
            src_ref=hx.at[:, src], dst_ref=hx.at[:, dst], send_sem=h_send.at[slot],
            recv_sem=h_recv.at[slot], device_id=(ax, to_rad), device_id_type=MESH)

    edge_out = edge(0, R, 0, rad + 1)
    edge_in = edge(1, 1, R + 1, rad - 1)
    pl.when(has_hi)(lambda: edge_out.start())
    pl.when(has_lo)(lambda: edge_in.start())

    @pl.when(rad == 0)
    def _():
        for c in range(3):
            for z in range(Z):
                hx[c, 0, z] = SIGNS[c] * SIGNS[1] * roll(hx[c, 1, z], half, 0)

    @pl.when(rad == n_rad - 1)
    def _():
        for c in range(3):
            for z in range(Z):
                hx[c, R + 1, z] = jnp.zeros((SUB, LANES), jnp.float32)

    bases, turns = [], []
    whole = [jnp.concatenate([below[c], mids[c], above[c]], axis=0)[:, 1:-1] for c in range(3)]
    for c in range(3):
        axial = mids[c] * mids[0]
        radial = whole[c] * whole[1]
        around = whole[c][1:-1] * whole[2][1:-1]
        change = axial[:, 2:] - axial[:, :-2] + (radial[2:] - radial[:-2]) + (up(around) - down(around))
        bases.append(whole[c][1:-1] - 0.5 * change)
        along = stress[pair(c, 0)]
        turn = stress[pair(c, 2)][:, 1:-1]
        turns.append(along[:, 2:] - along[:, :-2] + (up(turn) - down(turn)))

    count = n_ax * Z * T
    each(n_ax - 1, lambda i: sums_in(0, i + 1).wait_recv())

    def coefficients(total):
        total = jnp.broadcast_to(jnp.sum(jnp.where(group, total, 0.0), axis=1, keepdims=True), (SUB, LANES)) / count
        return total / (roll(total, -half, 0) + EPSILON)

    def total_of(side):
        first = first_of(side)
        total = part[...] if first else jnp.zeros((1, LANES), jnp.float32)
        if n_ax <= 16:
            for i in range(first, n_ax):
                total = total + parts[(1 + side) * n_ax + lax.rem(ax + i, n_ax)]
            return total
        return lax.fori_loop(
            first, n_ax, lambda i, t: t + parts[(1 + side) * n_ax + lax.rem(ax + i, n_ax)], total)

    coef = coefficients(total_of(0))

    def beside(side, row):
        each(n_ax, lambda i: sums_in(side, i).wait_recv())
        edge_coef[0 if side < 0 else 1] = jnp.broadcast_to(
            coefficients(total_of(side))[row : row + 1], (SUB, LANES))

    pl.when(has_lo)(lambda: beside(-1, R - 1))
    pl.when(has_hi)(lambda: beside(1, 0))

    @pl.when(rad == 0)
    def _():
        edge_coef[0] = jnp.broadcast_to(coef[0:1], (SUB, LANES))

    @pl.when(rad == n_rad - 1)
    def _():
        edge_coef[1] = jnp.zeros((SUB, LANES), jnp.float32)

    pl.when(has_lo)(lambda: edge_out.wait_recv())
    pl.when(has_hi)(lambda: edge_in.wait_recv())
    by_row = [edge_coef[0]] + [jnp.broadcast_to(coef[r : r + 1], (SUB, LANES)) for r in range(R)] + [edge_coef[1]]
    for c in range(3):
        for r in range(R):
            new = bases[c][r] + by_row[r + 1] * turns[c][r]
            new = new + (by_row[r + 2] * hx[c, r + 2] - by_row[r] * hx[c, r])
            for z in range(Z):
                row = ((c * R + r) * Z + z) * SUB
                own[row : row + SUB, :] = new[z]
    for c in range(3):
        for r in range(R):
            for k, tile in enumerate(joined(strips(c, r), wide, pad)):
                out_ref[c, r, :, k * LANES : (k + 1) * LANES] = tile

    wait_send([z_lo, z_hi])

    @pl.when(has_hi)
    def _():
        wait_send(out_going + [edge_out])
        each(n_ax, lambda i: sums(1, i).wait_send())

    @pl.when(has_lo)
    def _():
        wait_send(in_going + [edge_in])
        each(n_ax, lambda i: sums(-1, i).wait_send())

    each(n_ax - 1, lambda i: sums(0, i + 1).wait_send())


def shards(n_ax, n_rad, velocity, cycle_map):
    _, R, Z, T = velocity.shape
    return pl.pallas_call(
        functools.partial(kernel, n_ax, n_rad),
        out_shape=jax.ShapeDtypeStruct(velocity.shape, velocity.dtype),
        in_specs=[pl.BlockSpec(memory_space=pltpu.HBM)] * 2,
        out_specs=pl.BlockSpec(memory_space=pltpu.VMEM),
        scratch_shapes=[
            pltpu.VMEM(velocity.shape, jnp.float32),
            pltpu.VMEM(cycle_map.shape, jnp.int32),
            pltpu.VMEM((3 * R * Z * SUB, LANES), jnp.float32),
            pltpu.VMEM((2 * NRING * SUB, LANES), jnp.float32),
            pltpu.VMEM((3, R + 2, Z + 4, SUB, LANES), jnp.float32),
            pltpu.VMEM((3, R + 2, Z, SUB, LANES), jnp.float32),
            pltpu.VMEM((1, LANES), jnp.float32),
            pltpu.VMEM((3 * n_ax, 1, LANES), jnp.float32),
            pltpu.VMEM((2, SUB, LANES), jnp.float32),
            pltpu.VMEM((2, 3 * R * 2 * T // LANES, LANES), jnp.float32),
            pltpu.VMEM((2, 3 * R * 2 * T // LANES, LANES), jnp.float32),
            pltpu.VMEM((2 * 3 * R * 2 * SUB, LANES), jnp.float32),
            pltpu.SemaphoreType.REGULAR((len(stages(n_ax)),)),
            pltpu.SemaphoreType.DMA((2,)),
            pltpu.SemaphoreType.DMA((8,)),
            pltpu.SemaphoreType.DMA((8,)),
            pltpu.SemaphoreType.DMA((2,)),
            pltpu.SemaphoreType.DMA((2,)),
            pltpu.SemaphoreType.DMA((3 * n_ax,)),
            pltpu.SemaphoreType.DMA((3 * n_ax,)),
        ],
        compiler_params=pltpu.CompilerParams(collective_id=0, has_side_effects=True, vmem_limit_bytes=8 << 20),
    )(*(pltpu.with_memory_space_constraint(x, pltpu.HBM) for x in (velocity, cycle_map)))


def solution(mesh):
    n_ax, n_rad = mesh.shape["ax"], mesh.shape["rad"]
    spec = P(None, "rad", "ax", None)
    body = functools.partial(shards, n_ax, n_rad)
    return jax.shard_map(body, mesh=mesh, in_specs=(spec, P()), out_specs=spec, check_vma=False)
```

```python
import functools

import jax
import jax.numpy as jnp
from jax import lax
from jax.experimental import pallas as pl
from jax.experimental.pallas import tpu as pltpu
from jax.sharding import PartitionSpec as P

NRING = 3
MOSTSEG = 16
SUB = 8
LANES = 128
PAIRS = ((0, 0), (1, 1), (2, 2), (0, 1), (0, 2), (1, 2))
PAIR_WEIGHTS = (1.0, 1.0, 1.0, 2.0, 2.0, 2.0)
SIGNS = (1.0, -1.0, -1.0)
EPSILON = 1e-06
MESH = pl.DeviceIdType.MESH


def pair(a, b):
    return PAIRS.index((min(a, b), max(a, b)))


def each(count, body):
    if count <= 16:
        for i in range(count):
            body(i)
    else:
        lax.fori_loop(0, count, lambda i, c: (body(i), c)[1], 0)


def roll(x, shift, axis):
    size = x.shape[axis]
    return pltpu.roll(x, shift % size, axis)


def up(x):
    return roll(x, -1, x.ndim - 1)


def down(x):
    return roll(x, 1, x.ndim - 1)


def smooth_t(x):
    return (down(x) + 2.0 * x + up(x)) * 0.25


def smooth_z(x):
    return (x[:, :-2] + 2.0 * x[:, 1:-1] + x[:, 2:]) * 0.25


def tiles_of(x):
    return [x[:, k : k + LANES] for k in range(0, x.shape[1], LANES)]


def segments(x, wide, pad):
    rows, tiles = x[0].shape[0], len(x)
    total = tiles * LANES
    lane = lax.broadcasted_iota(jnp.int32, (rows, LANES), 1)
    pieces = []
    for s in range(SUB):
        start = (s * wide - pad) % total
        k, off = start // LANES, start % LANES
        first = x[k]
        if off:
            k2 = (k + 1) % tiles
            second = x[k2]
            first = jnp.where(lane < LANES - off, roll(first, -off, 1), roll(second, -off, 1))
        pieces.append(first)
    return pieces


def joined(pieces, wide, pad):
    rows = pieces[0].shape[0]
    lane = lax.broadcasted_iota(jnp.int32, (rows, LANES), 1)
    tiles = []
    for k in range(SUB * wide // LANES):
        lo, hi = k * LANES, (k + 1) * LANES
        s = lo // wide
        out = None
        while s * wide < hi:
            part = roll(pieces[s], s * wide - pad - lo, 1)
            out = part if out is None else jnp.where(lane >= s * wide - lo, part, out)
            s += 1
        tiles.append(out)
    return tiles


def strain(grads):
    tensor = []
    for c, a in PAIRS:
        if c == a:
            tensor.append(0.5 * grads[c][c])
        else:
            tensor.append(0.25 * (grads[c][a] + grads[a][c]))
    squares = sum(w * m * m for w, m in zip(PAIR_WEIGHTS, tensor))
    return tensor, jnp.sqrt(2.0 * squares)


def gradients(f):
    out = []
    for c in range(3):
        mid = f[c][1:-1, 1:-1]
        out.append(
            [
                f[c][1:-1, 2:] - f[c][1:-1, :-2],
                f[c][2:, 1:-1] - f[c][:-2, 1:-1],
                up(mid) - down(mid),
            ]
        )
    return out


def stages(n_ax):
    distances, own, beside = [1], 2, 1
    while own < n_ax // 2:
        distances.append(own)
        own, beside = 2 * own, beside + own
    while beside < n_ax // 2:
        distances.append(1)
        beside += 1
    return distances


def kernel(n_ax, n_rad, v_hbm, map_hbm, out_ref, nat, map_ref, own, maps, ext, hx, part, parts, edge_coef,
           z_out, z_in, z_seg, ready, in_sems, halo_send, halo_recv, h_send, h_recv, p_send, p_recv):
    rad = lax.axis_index("rad")
    ax = lax.axis_index("ax")
    R, Z, T = nat.shape[1], nat.shape[2], nat.shape[3]
    wide = T // SUB
    pad = (LANES - wide) // 2
    half = SUB // 2
    right, left = lax.rem(ax + 1, n_ax), lax.rem(ax + n_ax - 1, n_ax)
    has_lo, has_hi = rad > 0, rad < n_rad - 1

    def strips(c, r):
        return [own[pl.ds((c * R + r) * Z * SUB + s, Z, stride=SUB), :] for s in range(SUB)]

    barrier = pltpu.get_barrier_semaphore()

    def greet(to_ax, to_rad):
        pl.semaphore_signal(barrier, inc=1, device_id=(to_ax, to_rad), device_id_type=MESH)

    greet(left, rad)
    greet(right, rad)

    def greet_row(to_rad):
        for peer in (ax, left, right):
            greet(peer, to_rad)

    pl.when(has_lo)(lambda: greet_row(rad - 1))
    pl.when(has_hi)(lambda: greet_row(rad + 1))

    distances = stages(n_ax)

    def tell(stage):
        d = distances[stage]
        for peer in (lax.rem(ax + d, n_ax), lax.rem(ax + n_ax - d, n_ax)):
            pl.semaphore_signal(ready.at[stage], inc=1, device_id=(peer, rad), device_id_type=MESH)

    def hear(stage):
        pl.semaphore_wait(ready.at[stage], 2)

    fetch = pltpu.make_async_copy(v_hbm, nat, in_sems.at[0])
    fetch.start()
    fetch_map = pltpu.make_async_copy(map_hbm, map_ref, in_sems.at[1])
    pl.when(rad == 0)(lambda: fetch_map.start())
    fetch.wait()
    for c in range(3):
        for r in range(R):
            for s, piece in enumerate(segments(tiles_of(nat[c, r]), wide, pad)):
                own[pl.ds((c * R + r) * Z * SUB + s, Z, stride=SUB), :] = piece
    for c in range(3):
        for r in range(R):
            for z in range(Z):
                row = ((c * R + r) * Z + z) * SUB
                ext[c, r + 1, z + 2] = own[row : row + SUB, :]

    lane = lax.broadcasted_iota(jnp.int32, (SUB, LANES), 1)
    steps = []
    while 2 ** len(steps) < MOSTSEG:
        steps.append(2 ** len(steps))

    def cell_sums(r):
        label = maps[r * SUB : (r + 1) * SUB, :]
        before = [(roll(label, d, 1) == label).astype(jnp.float32) for d in steps]
        after = [(roll(label, -d, 1) == label).astype(jnp.float32) for d in steps]

        def spread(x):
            total, rest = x, x
            for d, b, a in zip(steps, before, after):
                total = total + b * roll(total, d, 1)
                rest = rest + a * roll(rest, -d, 1)
            return total + rest - x

        return spread

    def coarsen(r, spread, c, z):
        mean = spread(ext[c, r + 1, z]) * maps[(NRING + r) * SUB : (NRING + r + 1) * SUB, :]
        low = roll(roll(mean, -wide, 1), 1, 0)
        high = roll(roll(mean, wide, 1), -1, 0)
        mean = jnp.where(lane < pad, low, mean)
        ext[c, r + 1, z] = jnp.where(lane >= pad + wide, high, mean)

    @pl.when(rad == 0)
    def _():
        fetch_map.wait()
        labels = map_ref[...].astype(jnp.float32)
        for s, piece in enumerate(segments(tiles_of(labels), wide, pad)):
            maps[pl.ds(s, NRING, stride=SUB), :] = piece
        for r in range(NRING):
            spread = cell_sums(r)
            maps[(NRING + r) * SUB : (NRING + r + 1) * SUB, :] = 1.0 / spread(jnp.ones((SUB, LANES), jnp.float32))
            for c in range(3):
                for z in range(Z):
                    coarsen(r, spread, c, z + 2)
                    row = ((c * R + r) * Z + z) * SUB
                    own[row : row + SUB, :] = ext[c, r + 1, z + 2]
                for k, tile in enumerate(joined(strips(c, r), wide, pad)):
                    nat[c, r, :, k * LANES : (k + 1) * LANES] = tile

    n_rows = 3 * R * 2
    for side, first in ((0, Z - 2), (1, 0)):
        for c in range(3):
            for r in range(R):
                for k in range(T // LANES):
                    row = k * n_rows + (c * R + r) * 2
                    z_out[side, row : row + 2, :] = nat[c, r, first : first + 2, k * LANES : (k + 1) * LANES]

    pl.semaphore_wait(barrier, 2 + jnp.where(has_lo, 3, 0) + jnp.where(has_hi, 3, 0))

    def z_halo(slot, to_ax):
        return pltpu.make_async_remote_copy(
            src_ref=z_out.at[slot], dst_ref=z_in.at[slot], send_sem=halo_send.at[slot],
            recv_sem=halo_recv.at[slot], device_id=(to_ax, rad), device_id_type=MESH)

    z_lo, z_hi = z_halo(0, right), z_halo(1, left)
    z_lo.start()
    z_hi.start()
    tell(0)

    rows, cols = pl.ds(1, R), pl.ds(2, Z)

    def halo(slot, src, dst, to_ax, to_rad):
        return pltpu.make_async_remote_copy(
            src_ref=ext.at[src], dst_ref=ext.at[dst], send_sem=halo_send.at[slot],
            recv_sem=halo_recv.at[slot], device_id=(to_ax, to_rad), device_id_type=MESH)

    everything = slice(None)

    out_going = [
        halo(2, (everything, R, cols), (everything, 0, cols), ax, rad + 1),
        halo(3, (everything, R, Z + 1), (everything, 0, 1), right, rad + 1),
        halo(4, (everything, R, 2), (everything, 0, Z + 2), left, rad + 1),
    ]
    in_going = [
        halo(5, (everything, 1, cols), (everything, R + 1, cols), ax, rad - 1),
        halo(6, (everything, 1, Z + 1), (everything, R + 1, 1), right, rad - 1),
        halo(7, (everything, 1, 2), (everything, R + 1, Z + 2), left, rad - 1),
    ]

    def start_all(copies):
        for copy in copies:
            copy.start()

    def wait_recv(copies):
        for copy in copies:
            copy.wait_recv()

    def wait_send(copies):
        for copy in copies:
            copy.wait_send()

    pl.when(has_hi)(lambda: start_all(out_going))
    pl.when(has_lo)(lambda: start_all(in_going))
    for stage in range(len(distances) - 1)[:1]:
        hear(stage)
        tell(stage + 1)
    for side, copy, first in ((0, z_lo, 0), (1, z_hi, Z + 2)):
        copy.wait_recv()
        tiles = [z_in[side, k * n_rows : (k + 1) * n_rows, :] for k in range(T // LANES)]
        for s, piece in enumerate(segments(tiles, wide, pad)):
            z_seg[pl.ds(side * n_rows * SUB + s, n_rows, stride=SUB), :] = piece
        for c in range(3):
            for r in range(R):
                for z in range(2):
                    row = (side * n_rows + (c * R + r) * 2 + z) * SUB
                    ext[c, r + 1, first + z] = z_seg[row : row + SUB, :]
    for stage in range(1, len(distances) - 1):
        hear(stage)
        tell(stage + 1)

    long = [ext[c, 1 : R + 1, 0 : Z + 4] for c in range(3)]
    mids = [x[:, 1:-1] for x in long]
    grads, w_own, w_grads, leonards = [], [], [], []
    for c in range(3):
        turned = up(mids[c]) - down(mids[c])
        grads.append([long[c][:, 2:] - long[c][:, :-2], None, turned])
        w_own.append(smooth_t(smooth_z(long[c])))
        mid = w_own[c][:, 1:-1]
        w_grads.append([w_own[c][:, 2:] - w_own[c][:, :-2], None, up(mid) - down(mid)])
    for c, a in PAIRS:
        product = smooth_t(smooth_z(mids[c] * mids[a]))
        leonards.append(product - w_own[c][:, 1:-1] * w_own[a][:, 1:-1])

    pl.when(has_lo)(lambda: wait_recv(out_going))
    pl.when(has_hi)(lambda: wait_recv(in_going))

    @pl.when(rad == 0)
    def _():
        for c in range(3):
            for z in range(1, Z + 3):
                ext[c, 0, z] = SIGNS[c] * roll(ext[c, 1, z], half, 0)

    @pl.when(rad == n_rad - 1)
    def _():
        for c in range(3):
            for z in range(1, Z + 3):
                ext[c, R + 1, z] = jnp.zeros((SUB, LANES), jnp.float32)

    below = [ext[c, 0:1, 1 : Z + 3] for c in range(3)]
    above = [ext[c, R + 1 : R + 2, 1 : Z + 3] for c in range(3)]
    for c in range(3):
        column = jnp.concatenate([below[c], mids[c], above[c]], axis=0)
        grads[c][1] = column[2:] - column[:-2]
        column = jnp.concatenate(
            [smooth_t(smooth_z(below[c])), w_own[c][:, 1:-1], smooth_t(smooth_z(above[c]))], axis=0)
        w_grads[c][1] = column[2:] - column[:-2]
    tensor, mag = strain(grads)
    stress = [mag * t for t in tensor]
    w_tensor, w_mag = strain(w_grads)
    w_mag4 = 4.0 * w_mag
    lm, mm = 0.0, 0.0
    for number, leonard in enumerate(leonards):
        model = smooth_t(smooth_z(stress[number])) - w_mag4 * w_tensor[number]
        lm = lm + PAIR_WEIGHTS[number] * leonard * model
        mm = mm + PAIR_WEIGHTS[number] * model * model
    sub_index = lax.broadcasted_iota(jnp.int32, (SUB, LANES), 0)
    lane_index = lax.broadcasted_iota(jnp.int32, (SUB, LANES), 1)
    mine = jnp.zeros((SUB, LANES), jnp.float32)
    for r in range(R):
        for base, quantity in ((0, lm), (half, mm)):
            row = jnp.sum(jnp.sum(quantity[r], axis=0), axis=0, keepdims=True)
            mine = jnp.where(sub_index == base + r, row, mine)
    mine = jnp.where((lane_index >= pad) & (lane_index < pad + wide), mine, 0.0)
    fold = LANES // 2
    while fold >= LANES // SUB:
        mine = mine + roll(mine, fold, 1)
        fold //= 2
    group = lane_index // (LANES // SUB) == sub_index
    part[...] = jnp.sum(jnp.where(group, mine, 0.0), axis=0, keepdims=True)

    def sums(side, i):
        peer = lax.rem(ax + i, n_ax)
        return pltpu.make_async_remote_copy(
            src_ref=part, dst_ref=parts.at[(1 - side) * n_ax + ax],
            send_sem=p_send.at[(1 + side) * n_ax + i], recv_sem=p_recv.at[(1 - side) * n_ax + ax],
            device_id=(peer, rad + side), device_id_type=MESH)

    def sums_in(side, i):
        peer = lax.rem(ax + i, n_ax)
        slot = (1 + side) * n_ax + peer
        return pltpu.make_async_remote_copy(
            src_ref=part, dst_ref=parts.at[slot],
            send_sem=p_send.at[(1 + side) * n_ax + i], recv_sem=p_recv.at[slot],
            device_id=(peer, rad + side), device_id_type=MESH)

    def first_of(side):
        return 1 if side == 0 else 0

    def send_sums(side):
        first = first_of(side)
        each(n_ax - first, lambda i: sums(side, i + first).start())

    send_sums(0)
    hear(len(distances) - 1)
    pl.when(has_lo)(lambda: send_sums(-1))
    pl.when(has_hi)(lambda: send_sums(1))

    for c in range(3):
        hx[c, 1 : R + 1] = stress[pair(c, 1)][:, 1:-1]

    def edge(slot, src, dst, to_rad):
        return pltpu.make_async_remote_copy(
            src_ref=hx.at[:, src], dst_ref=hx.at[:, dst], send_sem=h_send.at[slot],
            recv_sem=h_recv.at[slot], device_id=(ax, to_rad), device_id_type=MESH)

    edge_out = edge(0, R, 0, rad + 1)
    edge_in = edge(1, 1, R + 1, rad - 1)
    pl.when(has_hi)(lambda: edge_out.start())
    pl.when(has_lo)(lambda: edge_in.start())

    @pl.when(rad == 0)
    def _():
        for c in range(3):
            for z in range(Z):
                hx[c, 0, z] = SIGNS[c] * SIGNS[1] * roll(hx[c, 1, z], half, 0)

    @pl.when(rad == n_rad - 1)
    def _():
        for c in range(3):
            for z in range(Z):
                hx[c, R + 1, z] = jnp.zeros((SUB, LANES), jnp.float32)

    bases, turns = [], []
    whole = [jnp.concatenate([below[c], mids[c], above[c]], axis=0)[:, 1:-1] for c in range(3)]
    for c in range(3):
        axial = mids[c] * mids[0]
        radial = whole[c] * whole[1]
        around = whole[c][1:-1] * whole[2][1:-1]
        change = axial[:, 2:] - axial[:, :-2] + (radial[2:] - radial[:-2]) + (up(around) - down(around))
        bases.append(whole[c][1:-1] - 0.5 * change)
        along = stress[pair(c, 0)]
        turn = stress[pair(c, 2)][:, 1:-1]
        turns.append(along[:, 2:] - along[:, :-2] + (up(turn) - down(turn)))

    count = n_ax * Z * T
    each(n_ax - 1, lambda i: sums_in(0, i + 1).wait_recv())

    def coefficients(total):
        total = jnp.broadcast_to(jnp.sum(jnp.where(group, total, 0.0), axis=1, keepdims=True), (SUB, LANES)) / count
        return total / (roll(total, -half, 0) + EPSILON)

    def total_of(side):
        first = first_of(side)
        total = part[...] if first else jnp.zeros((1, LANES), jnp.float32)
        if n_ax <= 16:
            for i in range(first, n_ax):
                total = total + parts[(1 + side) * n_ax + lax.rem(ax + i, n_ax)]
            return total
        return lax.fori_loop(
            first, n_ax, lambda i, t: t + parts[(1 + side) * n_ax + lax.rem(ax + i, n_ax)], total)

    coef = coefficients(total_of(0))

    def beside(side, row):
        each(n_ax, lambda i: sums_in(side, i).wait_recv())
        edge_coef[0 if side < 0 else 1] = jnp.broadcast_to(
            coefficients(total_of(side))[row : row + 1], (SUB, LANES))

    pl.when(has_lo)(lambda: beside(-1, R - 1))
    pl.when(has_hi)(lambda: beside(1, 0))

    @pl.when(rad == 0)
    def _():
        edge_coef[0] = jnp.broadcast_to(coef[0:1], (SUB, LANES))

    @pl.when(rad == n_rad - 1)
    def _():
        edge_coef[1] = jnp.zeros((SUB, LANES), jnp.float32)

    pl.when(has_lo)(lambda: edge_out.wait_recv())
    pl.when(has_hi)(lambda: edge_in.wait_recv())
    by_row = [edge_coef[0]] + [jnp.broadcast_to(coef[r : r + 1], (SUB, LANES)) for r in range(R)] + [edge_coef[1]]
    for c in range(3):
        for r in range(R):
            new = bases[c][r] + by_row[r + 1] * turns[c][r]
            new = new + (by_row[r + 2] * hx[c, r + 2] - by_row[r] * hx[c, r])
            for z in range(Z):
                row = ((c * R + r) * Z + z) * SUB
                own[row : row + SUB, :] = new[z]
    for c in range(3):
        for r in range(R):
            for k, tile in enumerate(joined(strips(c, r), wide, pad)):
                out_ref[c, r, :, k * LANES : (k + 1) * LANES] = tile

    wait_send([z_lo, z_hi])

    @pl.when(has_hi)
    def _():
        wait_send(out_going + [edge_out])
        each(n_ax, lambda i: sums(1, i).wait_send())

    @pl.when(has_lo)
    def _():
        wait_send(in_going + [edge_in])
        each(n_ax, lambda i: sums(-1, i).wait_send())

    each(n_ax - 1, lambda i: sums(0, i + 1).wait_send())


def shards(n_ax, n_rad, velocity, cycle_map):
    _, R, Z, T = velocity.shape
    return pl.pallas_call(
        functools.partial(kernel, n_ax, n_rad),
        out_shape=jax.ShapeDtypeStruct(velocity.shape, velocity.dtype),
        in_specs=[pl.BlockSpec(memory_space=pltpu.HBM)] * 2,
        out_specs=pl.BlockSpec(memory_space=pltpu.VMEM),
        scratch_shapes=[
            pltpu.VMEM(velocity.shape, jnp.float32),
            pltpu.VMEM(cycle_map.shape, jnp.int32),
            pltpu.VMEM((3 * R * Z * SUB, LANES), jnp.float32),
            pltpu.VMEM((2 * NRING * SUB, LANES), jnp.float32),
            pltpu.VMEM((3, R + 2, Z + 4, SUB, LANES), jnp.float32),
            pltpu.VMEM((3, R + 2, Z, SUB, LANES), jnp.float32),
            pltpu.VMEM((1, LANES), jnp.float32),
            pltpu.VMEM((3 * n_ax, 1, LANES), jnp.float32),
            pltpu.VMEM((2, SUB, LANES), jnp.float32),
            pltpu.VMEM((2, 3 * R * 2 * T // LANES, LANES), jnp.float32),
            pltpu.VMEM((2, 3 * R * 2 * T // LANES, LANES), jnp.float32),
            pltpu.VMEM((2 * 3 * R * 2 * SUB, LANES), jnp.float32),
            pltpu.SemaphoreType.REGULAR((len(stages(n_ax)),)),
            pltpu.SemaphoreType.DMA((2,)),
            pltpu.SemaphoreType.DMA((8,)),
            pltpu.SemaphoreType.DMA((8,)),
            pltpu.SemaphoreType.DMA((2,)),
            pltpu.SemaphoreType.DMA((2,)),
            pltpu.SemaphoreType.DMA((3 * n_ax,)),
            pltpu.SemaphoreType.DMA((3 * n_ax,)),
        ],
        compiler_params=pltpu.CompilerParams(collective_id=0, has_side_effects=True, vmem_limit_bytes=8 << 20),
    )(*(pltpu.with_memory_space_constraint(x, pltpu.HBM) for x in (velocity, cycle_map)))


def solution(mesh):
    n_ax, n_rad = mesh.shape["ax"], mesh.shape["rad"]
    spec = P(None, "rad", "ax", None)
    body = functools.partial(shards, n_ax, n_rad)
    return jax.shard_map(body, mesh=mesh, in_specs=(spec, P()), out_specs=spec, check_vma=False)
```
